256 devices in a mesh: row: 16 (over y, z_hi), col: 16 (over z_lo, x, core).
Axes of the slice: x: 4, y: 4, z: 8 (z_hi: 4, z_lo: 2; z = z_hi * 2 + z_lo), core: 2. Of those that a mesh axis runs over, the one named last changes fastest.
Arguments:
- features: bfloat16 [256, 256, 384], P('row', 'col'), may hold values from -6 to 6
- norm_gain: float32 [384], replicated, may hold values from 0.5 to 1.5
- in_weight: bfloat16 [384, 1536], replicated, may hold values from -0.3125 to 0.3125
- conv_weight: float32 [3, 3, 768], replicated, may hold values from -2 to 2
- conv_bias: float32 [768], replicated, may hold values from -3 to 3
- proj_weight: bfloat16 [4, 768, 56], replicated, may hold values from -0.21875 to 0.21875
- step_weight: float32 [4, 24, 768], replicated, may hold values from -1.25 to 1.25
- step_bias: float32 [4, 768], replicated, may hold values from -9 to 2
- decay_log: float32 [4, 768, 16], replicated, may hold values from -3 to 0
- skip_gain: float32 [4, 768], replicated, may hold values from 0.02 to 0.2
- out_gain: float32 [768], replicated, may hold values from 0.5 to 1.5
- out_weight: bfloat16 [768, 384], replicated, may hold values from -0.21875 to 0.21875
Outputs:
- block_out: bfloat16 [256, 256, 384], P('row', 'col')
The draws below stay inside these ranges and needn't reach their ends.
All inputs are finite; a program needn't handle non-finite values.
Results may differ from the reference program's by a relative error of at most 0.014.
Values may be sent and summed in bfloat16 or wider, within the bound.
A program may use at most 192 MiB of HBM per device.

```python
import jax
import jax.numpy as jnp
from jax import lax

C = 384
E = 768
N = 16
R = 24
IMG_H = 256
IMG_W = 256


def draw_step_bias(key, part):
    lengths = jnp.array([IMG_W, IMG_W, IMG_H, IMG_H], jnp.float32)[:, None]
    lowest, highest = (2.0, 100.0)
    picked = jax.random.uniform(key, (4, E), jnp.float32)
    base_step = jnp.exp(jnp.log(lowest) + picked * (jnp.log(highest) - jnp.log(lowest))) / lengths
    return jnp.log(jnp.expm1(base_step))


def steps_of(key, extent, cuts, low, top_value):
    gain = 1.0
    for position, parts in cuts:
        steps = jax.random.uniform(jax.random.fold_in(jax.random.fold_in(key, 6), position), (parts,), jnp.float32, low / len(cuts), top_value / len(cuts))
        gain = gain * jnp.repeat(jnp.exp(steps), extent[position] // parts).reshape((-1,) + (1,) * (len(extent) - 1 - position))
    return gain


def normal_values(stream_key, shape, width, reach, cuts=(), held_as=jnp.bfloat16):
    level = steps_of(stream_key, shape, cuts, -0.22, 0.18) if cuts else 1.0
    drawn = jax.random.normal(stream_key, shape, jnp.float32) * width * level
    return jnp.minimum(jnp.maximum(drawn, -reach), reach).astype(held_as)


def setup_inputs(seed: int = 0) -> dict:
    key_list = jax.random.split(jax.random.key(seed), 13)
    features = normal_values(key_list[0], (IMG_H, IMG_W, C), 1.0, 6.0, ((0, 16), (1, 16)))
    norm_gain = jnp.clip(1.0 + 0.1 * jax.random.normal(key_list[1], (C,), jnp.float32), 0.5, 1.5)
    in_weight = normal_values(key_list[2], (C, 2 * E), C ** -0.5, 0.3125)
    conv_weight = normal_values(key_list[3], (3, 3, E), 9 ** -0.5, 2.0, (), jnp.float32)
    conv_bias = normal_values(key_list[4], (E,), 0.5, 3.0, (), jnp.float32)
    proj_weight = normal_values(key_list[5], (4, E, R + 2 * N), E ** -0.5, 0.21875)
    step_weight = normal_values(key_list[6], (4, R, E), R ** -0.5, 1.25, (), jnp.float32)
    step_bias = draw_step_bias(jax.random.fold_in(key_list[12], 71), 0)
    decay_log = jnp.clip(jax.random.uniform(key_list[8], (4, E, N), jnp.float32, -3.0, 0.0), -3.0, 0.0)
    skip_gain = jnp.clip(jax.random.uniform(key_list[9], (4, E), jnp.float32, 0.02, 0.2), 0.02, 0.2)
    out_gain = jnp.clip(1.0 + 0.1 * jax.random.normal(key_list[10], (E,), jnp.float32), 0.5, 1.5)
    out_weight = normal_values(key_list[11], (E, C), E ** -0.5, 0.21875)
    return dict(features=features, norm_gain=norm_gain, in_weight=in_weight, conv_weight=conv_weight, conv_bias=conv_bias, proj_weight=proj_weight, step_weight=step_weight, step_bias=step_bias, decay_log=decay_log, skip_gain=skip_gain, out_gain=out_gain, out_weight=out_weight)


def layer_norm(values, scale_gain):
    centred = values - lax.optimization_barrier(jnp.mean(values, axis=-1, keepdims=True))
    spread = lax.optimization_barrier(jnp.mean(centred * centred, axis=-1, keepdims=True))
    return centred * lax.rsqrt(spread + 1e-05) * scale_gain

def line_scan(line_input, proj_part, step_part, bias_part, decay_part, skip_part, reverse):
    rank_size = step_part.shape[0]
    state_size = decay_part.shape[1]
    widened = line_input.astype(jnp.float32)
    projected = jnp.einsum('lpe,ef->lpf', widened, proj_part.astype(jnp.float32))
    step_size = jax.nn.softplus(jnp.einsum('lpr,re->lpe', projected[..., :rank_size], step_part, precision=lax.Precision.HIGHEST) + bias_part)
    enter_coef = projected[..., rank_size:rank_size + state_size]
    leave_coef = projected[..., rank_size + state_size:]
    decay_rate = -jnp.exp(decay_part)

    def advance(hidden_state, pieces):
        step_now, input_now, enter_now, leave_now = pieces
        hidden_state = jnp.exp(step_now[:, :, None] * decay_rate) * hidden_state + (step_now * input_now)[:, :, None] * enter_now[:, None, :]
        return (hidden_state, lax.optimization_barrier(jnp.sum(hidden_state * leave_now[:, None, :], axis=-1)))
    sliced = tuple((jnp.moveaxis(member, 1, 0) for member in (step_size, widened, enter_coef, leave_coef)))
    initial = jnp.zeros((line_input.shape[0], line_input.shape[2], state_size), jnp.float32)
    _, outputs = lax.scan(advance, initial, sliced, reverse=reverse)
    return jnp.moveaxis(outputs, 0, 1) + skip_part * widened

def reference(features, norm_gain, in_weight, conv_weight, conv_bias, proj_weight, step_weight, step_bias, decay_log, skip_gain, out_gain, out_weight):
    height, breadth, channels = features.shape
    inner_width = out_weight.shape[0]
    normed = layer_norm(features.astype(jnp.float32), norm_gain).astype(jnp.bfloat16)
    mixed_proj = jnp.dot(normed.reshape(height * breadth, channels), in_weight, preferred_element_type=jnp.float32).reshape(height, breadth, 2 * inner_width)
    inner_part = mixed_proj[..., :inner_width].astype(jnp.bfloat16)
    gate_part = mixed_proj[..., inner_width:].astype(jnp.bfloat16)
    padded = jnp.pad(inner_part.astype(jnp.float32), ((1, 1), (1, 1), (0, 0)))
    summed = jnp.zeros((height, breadth, inner_width), jnp.float32) + conv_bias
    for tap_row in range(3):
        for tap_col in range(3):
            summed = summed + padded[tap_row:tap_row + height, tap_col:tap_col + breadth] * conv_weight[tap_row, tap_col]
    activated = jax.nn.silu(summed).astype(jnp.bfloat16)
    transposed = jnp.swapaxes(activated, 0, 1)

    def direction(line_input, which_dir, reverse):
        return line_scan(line_input, proj_weight[which_dir], step_weight[which_dir], step_bias[which_dir], decay_log[which_dir], skip_gain[which_dir], reverse)
    row_part = direction(activated, 0, False) + direction(activated, 1, True)
    column_part = direction(transposed, 2, False) + direction(transposed, 3, True)
    combined = row_part + jnp.swapaxes(column_part, 0, 1)
    gated_out = (layer_norm(combined, out_gain) * jax.nn.silu(gate_part.astype(jnp.float32))).astype(jnp.bfloat16)
    block_out = jnp.dot(gated_out.reshape(height * breadth, inner_width), out_weight, preferred_element_type=jnp.float32)
    return block_out.astype(jnp.bfloat16).reshape(height, breadth, channels)
```

```python
import functools

import jax
import jax.numpy as jnp
from jax import lax
from jax.experimental import pallas as pl
from jax.experimental.pallas import tpu as pltpu
from jax.sharding import PartitionSpec as P

F32 = jnp.float32
BF16 = jnp.bfloat16
MESH = pl.DeviceIdType.MESH
NT = (((1,), (1,)), ((), ()))
LANES = 128
LOG2E = 1.4426950408889634
VMEM = pl.BlockSpec(memory_space=pltpu.VMEM)


def dot(a, b):
    return jnp.dot(a, b, preferred_element_type=F32)


def dot_nt(a, b):
    return lax.dot_general(a, b, NT, preferred_element_type=F32)


def softplus(z):
    w = jnp.exp2(jnp.abs(z) * -LOG2E)
    small = w * (1.0 - w * (0.5 - w * (1.0 / 3.0)))
    return jnp.maximum(z, 0.0) + jnp.where(w < 0.01, small, jnp.log(1.0 + w))


def silu(v):
    return v / (1.0 + jnp.exp(-v))


def iota(shape, dim):
    return lax.broadcasted_iota(jnp.int32, shape, dim)


def cols(k):
    return slice(k * LANES, (k + 1) * LANES)


def place():
    return lax.axis_index("row"), lax.axis_index("col")


def greet(nr, nc, corners):
    row, col = place()
    sem = pltpu.get_barrier_semaphore()
    count = 0

    def signal(r, c):
        pl.semaphore_signal(sem, inc=1, device_id={"row": r, "col": c}, device_id_type=MESH)

    def along_col(k, _):
        signal(row, lax.rem(col + k, nc))
        return 0

    def along_row(k, _):
        signal(lax.rem(row + k, nr), col)
        return 0

    lax.fori_loop(1, nc, along_col, 0)
    lax.fori_loop(1, nr, along_row, 0)
    count = nc - 1 + nr - 1
    if corners:
        for dr in (1, nr - 1):
            for dc in (1, nc - 1):
                signal(lax.rem(row + dr, nr), lax.rem(col + dc, nc))
                count += 1
    return lambda: pl.semaphore_wait(sem, count)


def exchange(nr, nc, source, target, send_sem, recv_sem):
    row, col = place()

    def copy(axis, peer, owner, step):
        device = {"row": row, "col": peer} if axis == 0 else {"row": peer, "col": col}
        return pltpu.make_async_remote_copy(
            src_ref=source(axis, peer),
            dst_ref=target(axis, owner),
            send_sem=send_sem.at[axis, step],
            recv_sem=recv_sem.at[axis, owner],
            device_id=device,
            device_id_type=MESH,
        )

    def start(axis):
        me, count = ((col, nc), (row, nr))[axis]

        def one(step, _):
            copy(axis, lax.rem(me + step, count), me, step).start()
            return 0

        lax.fori_loop(1, count, one, 0)

    def wait(axis):
        me, count = ((col, nc), (row, nr))[axis]

        def one(step, _):
            peer = lax.rem(me + step, count)
            copy(axis, peer, me, step).wait_send()
            copy(axis, peer, peer, step).wait_recv()
            return 0

        lax.fori_loop(1, count, one, 0)

    return start, wait


def front_kernel(
    nr, nc, x_ref, gain_ref, wi_ref, cw_ref, cb_ref, gate_ref, lines_ref,
    nb_ref, nf_ref, strip_ref, halo_ref, pad_ref, act_ref, actt_ref, actf_ref, land_ref,
    hs_sem, hr_sem, send_sem, recv_sem,
):
    tr, tc, channels = x_ref.shape
    width = cb_ref.shape[1]
    tokens = tr * tc
    groups = width // LANES
    row, col = place()
    greeted = greet(nr, nc, True)

    step = 4 * tc

    def norm(i, _):
        v = x_ref[pl.ds(i * 4, 4)].reshape(step, channels).astype(F32)
        v = v - jnp.mean(v, axis=-1, keepdims=True)
        v = v * lax.rsqrt(jnp.mean(v * v, axis=-1, keepdims=True) + 1e-05) * gain_ref[...]
        at = pl.ds(pl.multiple_of(i * step, step), step)
        nb_ref[at, :] = v.astype(BF16)
        for k in range(channels // LANES):
            nf_ref[k, at, :] = v[:, cols(k)]
        return 0

    lax.fori_loop(0, tokens // step, norm, 0)
    for k in range(channels // LANES):
        strip_ref[0, :, cols(k)] = nf_ref[k, pl.ds(0, tr, stride=tc), :].astype(BF16)
        strip_ref[1, :, cols(k)] = nf_ref[k, pl.ds(tc - 1, tr, stride=tc), :].astype(BF16)
    top, bottom = nb_ref.at[pl.ds(0, tc)], nb_ref.at[pl.ds(tokens - tc, tc)]
    left, right = strip_ref.at[0], strip_ref.at[1]
    up, down = lax.rem(row + nr - 1, nr), lax.rem(row + 1, nr)
    west, east = lax.rem(col + nc - 1, nc), lax.rem(col + 1, nc)
    greeted()
    plan = (
        (bottom, down, col), (top, up, col), (right, row, east), (left, row, west),
        (bottom, down, east), (bottom, down, west), (top, up, east), (top, up, west),
    )
    halos = []
    for slot, (src, r, c) in enumerate(plan):
        halos.append(
            pltpu.make_async_remote_copy(
                src_ref=src, dst_ref=halo_ref.at[pl.ds(slot * tc, tc)],
                send_sem=hs_sem.at[slot], recv_sem=hr_sem.at[slot],
                device_id={"row": r, "col": c}, device_id_type=MESH,
            )
        )
        halos[-1].start()

    def project(i, _):
        at = pl.ds(pl.multiple_of(i * step, step), step)
        mixed = dot(nb_ref[at, :], wi_ref[...])
        gate_ref[at, :] = mixed[:, width:].astype(BF16)
        inner = mixed[:, :width].astype(BF16).astype(F32)
        for k in range(groups):
            pad_ref[k, pl.ds(1 + i * 4, 4), 8 : 8 + tc, :] = inner[:, cols(k)].reshape(4, tc, LANES)
        return 0

    lax.fori_loop(0, tokens // step, project, 0)
    for copy in halos:
        copy.wait()
    edge = dot(halo_ref[...], wi_ref[:, :width]).astype(BF16).astype(F32)
    north, south = row > 0, row < nr - 1
    lwest, least = col > 0, col < nc - 1

    def seen(slot, ok, first=0, count=None):
        part = edge[slot * tc + first : slot * tc + first + (tc if count is None else count)]
        return jnp.where(ok, part, 0.0)

    n_all, s_all = seen(0, north), seen(1, south)
    w_all, e_all = seen(2, lwest), seen(3, least)
    nw, ne = seen(4, north & lwest, tc - 8, 8), seen(5, north & least, 0, 8)
    sw, se = seen(6, south & lwest, tc - 8, 8), seen(7, south & least, 0, 8)
    for k in range(groups):
        pad_ref[k, 0, 8 : 8 + tc, :] = n_all[:, cols(k)]
        pad_ref[k, tr + 1, 8 : 8 + tc, :] = s_all[:, cols(k)]
        pad_ref[k, 0, 0:8, :] = nw[:, cols(k)]
        pad_ref[k, 0, 8 + tc : 16 + tc, :] = ne[:, cols(k)]
        pad_ref[k, tr + 1, 0:8, :] = sw[:, cols(k)]
        pad_ref[k, tr + 1, 8 + tc : 16 + tc, :] = se[:, cols(k)]
        for r in range(tr):
            pad_ref[k, 1 + r, 7:8, :] = w_all[r : r + 1, cols(k)]
            pad_ref[k, 1 + r, 8 + tc : 9 + tc, :] = e_all[r : r + 1, cols(k)]

    def convolve(r, _):
        for k in range(groups):
            total = jnp.broadcast_to(cb_ref[:, cols(k)], (tc, LANES))
            for a in range(3):
                for b in range(3):
                    total = total + pad_ref[k, r + a, 7 + b : 7 + b + tc, :] * cw_ref[a, b : b + 1, cols(k)]
            done = silu(total).astype(BF16)
            act_ref[r, :, cols(k)] = done
            actf_ref[k, pl.ds(pl.multiple_of(r * tc, tc), tc), :] = done.astype(F32)
        return 0

    lax.fori_loop(0, tr, convolve, 0)

    def source(axis, peer):
        return act_ref.at[peer] if axis == 0 else actt_ref.at[peer]

    def target(axis, owner):
        return land_ref.at[axis, pl.ds(pl.multiple_of(owner * tc, tc), tc)]

    start, wait = exchange(nr, nc, source, target, send_sem, recv_sem)
    start(0)

    def flip(j, _):
        for k in range(groups):
            actt_ref[j, :, cols(k)] = actf_ref[k, pl.ds(j, tr, stride=tc), :].astype(BF16)
        return 0

    lax.fori_loop(0, tc, flip, 0)
    start(1)
    land_ref[0, pl.ds(pl.multiple_of(col * tc, tc), tc), :] = act_ref[col]
    land_ref[1, pl.ds(pl.multiple_of(row * tr, tr), tr), :] = actt_ref[row]
    wait(0)
    wait(1)
    lines_ref[...] = land_ref[...]


def scan_kernel(
    chunk, u_ref, pw_ref, sw_ref, sb_ref, dl_ref, sk_ref, y_ref,
    ph_ref, pl_ref, s_ref, du_ref, bb_ref, mc_ref, dec_ref, ha_ref, hb_ref, acc_ref,
):
    length, width = u_ref.shape
    rank = sw_ref.shape[1]
    states = dl_ref.shape[1]
    parts = pw_ref.shape[1]
    span = 16
    line = pl.program_id(0)
    held = (ha_ref, hb_ref)
    kk, cc = iota((parts, span * states), 0), iota((parts, span * states), 1)
    repeat = (kk == rank + states + lax.rem(cc, states)).astype(BF16)
    mask = lax.rem(iota((length, span * states), 0), span) == iota((length, span * states), 1) // states
    ones = jnp.ones((LANES, LANES), BF16)
    lane = iota((states, LANES), 1)

    def prepare(d, _):
        p = dot_nt(u_ref[...], pw_ref[d])
        high = p.astype(BF16)
        ph_ref[d] = high
        pl_ref[d] = (p - high.astype(F32)).astype(BF16)
        mc_ref[d] = jnp.where(mask, dot(high, repeat), 0.0).astype(BF16)
        enter = dot_nt(pw_ref[d, rank : rank + states, :], u_ref[...])
        for h in range(length // LANES):
            for g in range(0, LANES, span):
                spread = [jnp.where(lane == g + i, enter[:, cols(h)], 0.0) for i in range(span)]
                at = (h * LANES + g) * states
                bb_ref[d, at : at + span * states, :] = dot(jnp.concatenate(spread, axis=0).astype(BF16), ones)
        dec_ref[d] = jnp.exp(dl_ref[d]) * -LOG2E
        sw = sw_ref[d]
        swh = sw.astype(BF16)
        swl = (sw - swh.astype(F32)).astype(BF16)
        bias = sb_ref[pl.ds(line * 2 + d, 1), :]

        def step_size(i, _):
            at = pl.ds(pl.multiple_of(i * 32, 32), 32)
            a = ph_ref[d, at, :rank]
            s = softplus(dot(a, swh) + (dot(a, swl) + dot(pl_ref[d, at, :rank], swh)) + bias)
            du = s * u_ref[at, :].astype(F32)
            for k in range(width // LANES):
                s_ref[d, k, at, :] = s[:, cols(k)]
                du_ref[d, k, at, :] = du[:, cols(k)]
            return 0

        lax.fori_loop(0, length // 32, step_size, 0)
        return 0

    lax.fori_loop(0, 2, prepare, 0)
    skip = sk_ref[pl.ds(line * 2, 1), :] + sk_ref[pl.ds(line * 2 + 1, 1), :]

    def begin(i, _):
        at = pl.ds(pl.multiple_of(i * 32, 32), 32)
        acc_ref[at, :] = u_ref[at, :].astype(F32) * skip
        return 0

    lax.fori_loop(0, length // 32, begin, 0)
    blocks = length // span
    per = chunk // LANES

    for g0 in range(0, width // LANES, per):
        c0 = g0 * LANES
        dec = [[[dec_ref[d, 8 * v : 8 * v + 8, cols(g0 + k)] for v in range(2)] for k in range(per)] for d in range(2)]

        def leave(slot, i, d):
            b = pl.multiple_of((i if d == 0 else blocks - 1 - i) * span, span)
            states_now = jnp.concatenate([held[slot][d, k] for k in range(per)], axis=1)
            acc_ref[pl.ds(b, span), c0 : c0 + chunk] += dot(mc_ref[d, pl.ds(b, span), :], states_now)

        def advance(slot, i, h):
            base = (i * span, (blocks - 1 - i) * span)
            for j in range(span):
                for d in range(2):
                    jj = j if d == 0 else span - 1 - j
                    t = base[d] + jj
                    enter = [bb_ref[d, pl.ds(pl.multiple_of(t * states + 8 * v, 8), 8), :] for v in range(2)]
                    for k in range(per):
                        s = s_ref[d, g0 + k, pl.ds(t, 8, stride=0), :]
                        du = du_ref[d, g0 + k, pl.ds(t, 8, stride=0), :]
                        now = [jnp.exp2(s * dec[d][k][v]) * h[d][k][v] + du * enter[v] for v in range(2)]
                        h[d][k] = now
                        held[slot][d, k, jj * states : (jj + 1) * states, :] = jnp.concatenate(now, axis=0).astype(BF16)
            return h

        def body(i, h):
            h = [[list(v) for v in part] for part in h]
            for d in range(2):
                leave(1, jnp.maximum(2 * i - 1, 0), d)
            h = advance(0, 2 * i, h)
            for d in range(2):
                leave(0, 2 * i, d)
            h = advance(1, 2 * i + 1, h)
            return tuple(tuple(tuple(v) for v in part) for part in h)

        hb_ref[...] = jnp.zeros_like(hb_ref)
        zero = jnp.zeros((8, LANES), F32)
        lax.fori_loop(0, blocks // 2, body, tuple(tuple((zero, zero) for _ in range(per)) for _ in range(2)))
        for d in range(2):
            leave(1, blocks - 1, d)
    y_ref[...] = acc_ref[...].astype(BF16)


def back_kernel(
    nr, nc, y_ref, gate_ref, gain_ref, wo_ref, out_ref, land_ref, cf_ref, go_ref, send_sem, recv_sem,
):
    tr, tc, _ = out_ref.shape
    width = wo_ref.shape[0]
    groups = width // LANES
    row, col = place()
    greet(nr, nc, False)()

    def source(axis, peer):
        return y_ref.at[axis, pl.ds(pl.multiple_of(peer * tc, tc), tc)]

    def target(axis, owner):
        return land_ref.at[axis, owner]

    start, wait = exchange(nr, nc, source, target, send_sem, recv_sem)
    start(0)
    start(1)
    land_ref[0, col] = y_ref[0, pl.ds(pl.multiple_of(col * tc, tc), tc), :]
    land_ref[1, row] = y_ref[1, pl.ds(pl.multiple_of(row * tr, tr), tr), :]
    wait(0)
    wait(1)

    def widen(j, _):
        for k in range(groups):
            cf_ref[k, pl.ds(pl.multiple_of(j * tr, tr), tr), :] = land_ref[1, j, :, cols(k)].astype(F32)
        return 0

    lax.fori_loop(0, tc, widen, 0)

    def finish(r, _):
        other = jnp.concatenate([cf_ref[k, pl.ds(r, tc, stride=tr), :] for k in range(groups)], axis=1)
        v = land_ref[0, r].astype(F32) + other
        v = v - jnp.mean(v, axis=-1, keepdims=True)
        v = v * lax.rsqrt(jnp.mean(v * v, axis=-1, keepdims=True) + 1e-05) * gain_ref[...]
        at = pl.ds(pl.multiple_of(r * tc, tc), tc)
        go_ref[at, :] = (v * silu(gate_ref[at, :].astype(F32))).astype(BF16)
        return 0

    lax.fori_loop(0, tr, finish, 0)
    out_ref[...] = dot(go_ref[...], wo_ref[...]).astype(BF16).reshape(out_ref.shape)


def local(
    nr, nc, features, norm_gain, in_weight, conv_weight, conv_bias, proj_weight, step_weight, step_bias,
    decay_log, skip_gain, out_gain, out_weight,
):
    tr, tc, channels = features.shape
    width = out_weight.shape[0]
    tokens = tr * tc
    groups = width // LANES
    length = tc * nc
    dma = pltpu.SemaphoreType.DMA
    gate, lines = pl.pallas_call(
        functools.partial(front_kernel, nr, nc),
        out_shape=(
            jax.ShapeDtypeStruct((tokens, width), BF16),
            jax.ShapeDtypeStruct((2, length, width), BF16),
        ),
        in_specs=[VMEM] * 5,
        out_specs=(VMEM, VMEM),
        scratch_shapes=[
            pltpu.VMEM((tokens, channels), BF16),
            pltpu.VMEM((channels // LANES, tokens, LANES), F32),
            pltpu.VMEM((2, tr, channels), BF16),
            pltpu.VMEM((8 * tc, channels), BF16),
            pltpu.VMEM((groups, tr + 2, tc + 16, LANES), F32),
            pltpu.VMEM((tr, tc, width), BF16),
            pltpu.VMEM((tc, tr, width), BF16),
            pltpu.VMEM((groups, tokens, LANES), F32),
            pltpu.VMEM((2, length, width), BF16),
            dma((8,)), dma((8,)), dma((2, nc)), dma((2, nc)),
        ],
        compiler_params=pltpu.CompilerParams(collective_id=0, has_side_effects=True, vmem_limit_bytes=40 << 20),
    )(features, norm_gain[None], in_weight, conv_weight, conv_bias[None])

    pw = jnp.swapaxes(proj_weight, 1, 2)
    dl = jnp.swapaxes(decay_log, 1, 2)
    rank, states = step_weight.shape[1], dl.shape[1]
    span, chunk = 16, 256
    pair = lambda a: pl.BlockSpec((2,) + a.shape[1:], lambda i: (i,) + (0,) * (a.ndim - 1))
    whole = lambda a: pl.BlockSpec(a.shape, lambda i: (0,) * a.ndim)
    y = pl.pallas_call(
        functools.partial(scan_kernel, chunk),
        out_shape=jax.ShapeDtypeStruct((2, length, width), BF16),
        grid=(2,),
        in_specs=[
            pl.BlockSpec((None, length, width), lambda i: (i, 0, 0)),
            pair(pw), pair(step_weight), whole(step_bias), pair(dl), whole(skip_gain),
        ],
        out_specs=pl.BlockSpec((None, length, width), lambda i: (i, 0, 0)),
        scratch_shapes=[
            pltpu.VMEM((2, length, pw.shape[1]), BF16),
            pltpu.VMEM((2, length, pw.shape[1]), BF16),
            pltpu.VMEM((2, groups, length, LANES), F32),
            pltpu.VMEM((2, groups, length, LANES), F32),
            pltpu.VMEM((2, length * states, LANES), F32),
            pltpu.VMEM((2, length, span * states), BF16),
            pltpu.VMEM((2, states, width), F32),
            pltpu.VMEM((2, chunk // LANES, span * states, LANES), BF16),
            pltpu.VMEM((2, chunk // LANES, span * states, LANES), BF16),
            pltpu.VMEM((length, width), F32),
        ],
        compiler_params=pltpu.CompilerParams(vmem_limit_bytes=48 << 20),
    )(lines, pw, step_weight, step_bias, dl, skip_gain)

    return pl.pallas_call(
        functools.partial(back_kernel, nr, nc),
        out_shape=jax.ShapeDtypeStruct(features.shape, BF16),
        in_specs=[VMEM] * 4,
        out_specs=VMEM,
        scratch_shapes=[
            pltpu.VMEM((2, tc, tr, width), BF16),
            pltpu.VMEM((groups, tokens, LANES), F32),
            pltpu.VMEM((tokens, width), BF16),
            dma((2, nc)), dma((2, nc)),
        ],
        compiler_params=pltpu.CompilerParams(collective_id=1, has_side_effects=True, vmem_limit_bytes=40 << 20),
    )(y, gate, out_gain[None], out_weight)


def solution(mesh):
    nr, nc = mesh.shape["row"], mesh.shape["col"]
    in_specs = (P("row", "col", None), P(), P(), P(), P(), P(), P(), P(), P(), P(), P(), P())
    return jax.shard_map(
        functools.partial(local, nr, nc), mesh=mesh, in_specs=in_specs, out_specs=P("row", "col", None), check_vma=False
    )
```

```python
import functools

import jax
import jax.numpy as jnp
from jax import lax
from jax.experimental import pallas as pl
from jax.experimental.pallas import tpu as pltpu
from jax.sharding import PartitionSpec as P

F32 = jnp.float32
BF16 = jnp.bfloat16
MESH = pl.DeviceIdType.MESH
NT = (((1,), (1,)), ((), ()))
LANES = 128
LOG2E = 1.4426950408889634
VMEM = pl.BlockSpec(memory_space=pltpu.VMEM)


def dot(a, b):
    return jnp.dot(a, b, preferred_element_type=F32)


def dot_nt(a, b):
    return lax.dot_general(a, b, NT, preferred_element_type=F32)


def softplus(z):
    w = jnp.exp2(jnp.abs(z) * -LOG2E)
    small = w * (1.0 - w * (0.5 - w * (1.0 / 3.0)))
    return jnp.maximum(z, 0.0) + jnp.where(w < 0.01, small, jnp.log(1.0 + w))


def silu(v):
    return v / (1.0 + jnp.exp(-v))


def iota(shape, dim):
    return lax.broadcasted_iota(jnp.int32, shape, dim)


def cols(k):
    return slice(k * LANES, (k + 1) * LANES)


def place():
    return lax.axis_index("row"), lax.axis_index("col")


def greet(nr, nc):
    row, col = place()
    sem = pltpu.get_barrier_semaphore()

    def signal(r, c):
        pl.semaphore_signal(sem, inc=1, device_id={"row": r, "col": c}, device_id_type=MESH)

    def along_col(k, _):
        signal(row, lax.rem(col + k, nc))
        return 0

    def along_row(k, _):
        signal(lax.rem(row + k, nr), col)
        return 0

    lax.fori_loop(1, nc, along_col, 0)
    lax.fori_loop(1, nr, along_row, 0)
    for dr in (1, nr - 1):
        for dc in (1, nc - 1):
            signal(lax.rem(row + dr, nr), lax.rem(col + dc, nc))
    return lambda: pl.semaphore_wait(sem, nr + nc + 2)


def remote(src, dst, send_sem, recv_sem, r, c):
    return pltpu.make_async_remote_copy(
        src_ref=src, dst_ref=dst, send_sem=send_sem, recv_sem=recv_sem,
        device_id={"row": r, "col": c}, device_id_type=MESH,
    )


def block_kernel(
    n, per, x_hbm, gain_ref, wi_hbm, cw_ref, cb_ref, pw_hbm, sw_hbm, sb_ref, dl_hbm, sk_ref, og_ref, wo_hbm, out_ref,
    x_ref, wi_ref, pw_ref, sw_ref, dl_ref, wo_ref,
    nb_ref, nf_ref, strip_ref, halo_ref, pad_ref, act_ref, actt_ref, actf_ref, line_ref, gate_ref,
    ph_ref, pl_ref, s_ref, du_ref, bb_ref, mc_ref, dec_ref, ha_ref, hb_ref, acc_ref, y_ref, land_ref, cf_ref, go_ref,
    own_sem, hs_sem, hr_sem, ts_sem, tr_sem, ys_sem, yr_sem,
):
    tr, tc, channels = x_ref.shape
    width = cb_ref.shape[-1]
    tokens = tr * tc
    groups = width // LANES
    chunks = groups // per
    chunk = per * LANES
    length = line_ref.shape[1]
    rank, states, parts = sw_ref.shape[1], dl_ref.shape[1], pw_ref.shape[1]
    row, col = place()
    fetch = [
        pltpu.make_async_copy(src, dst, own_sem.at[i])
        for i, (src, dst) in enumerate(
            ((x_hbm, x_ref), (wi_hbm, wi_ref), (pw_hbm, pw_ref), (sw_hbm, sw_ref), (dl_hbm, dl_ref), (wo_hbm, wo_ref))
        )
    ]
    for copy in fetch:
        copy.start()
    greeted = greet(n, n)

    def mine(axis):
        return col + axis * (row - col)

    def across(axis, peer):
        return row + axis * (peer - row), peer + axis * (col - peer)

    def every(axis, one):
        me = mine(axis)

        def body(step, _):
            one(step, lax.rem(me + step, n))
            return 0

        lax.fori_loop(1, n, body, 0)

    def tile(i):
        return pl.ds(pl.multiple_of(i * tc, tc), tc)

    step = 4 * tc
    fetch[0].wait()

    def norm(i, _):
        v = x_ref[pl.ds(i * 4, 4)].reshape(step, channels).astype(F32)
        v = v - jnp.mean(v, axis=-1, keepdims=True)
        v = v * lax.rsqrt(jnp.mean(v * v, axis=-1, keepdims=True) + 1e-05) * gain_ref[...].reshape(1, channels)
        at = pl.ds(pl.multiple_of(i * step, step), step)
        nb_ref[at, :] = v.astype(BF16)
        for k in range(channels // LANES):
            nf_ref[k, at, :] = v[:, cols(k)]
        return 0

    lax.fori_loop(0, tokens // step, norm, 0)
    for k in range(channels // LANES):
        strip_ref[0, :, cols(k)] = nf_ref[k, pl.ds(0, tr, stride=tc), :].astype(BF16)
        strip_ref[1, :, cols(k)] = nf_ref[k, pl.ds(tc - 1, tr, stride=tc), :].astype(BF16)
    top, bottom = nb_ref.at[pl.ds(0, tc)], nb_ref.at[pl.ds(tokens - tc, tc)]
    left, right = strip_ref.at[0], strip_ref.at[1]
    up, down = lax.rem(row + n - 1, n), lax.rem(row + 1, n)
    west, east = lax.rem(col + n - 1, n), lax.rem(col + 1, n)
    greeted()
    plan = (
        (bottom, down, col), (top, up, col), (right, row, east), (left, row, west),
        (bottom, down, east), (bottom, down, west), (top, up, east), (top, up, west),
    )
    halos = [
        remote(src, halo_ref.at[pl.ds(slot * tc, tc)], hs_sem.at[slot], hr_sem.at[slot], r, c)
        for slot, (src, r, c) in enumerate(plan)
    ]
    for copy in halos:
        copy.start()
    fetch[1].wait()

    def project(i, _):
        at = pl.ds(pl.multiple_of(i * step, step), step)
        inner = dot(nb_ref[at, :], wi_ref[:, :width]).astype(BF16).astype(F32)
        for k in range(groups):
            pad_ref[k, pl.ds(1 + i * 4, 4), 8 : 8 + tc, :] = inner[:, cols(k)].reshape(4, tc, LANES)
        return 0

    lax.fori_loop(0, tokens // step, project, 0)
    for copy in halos:
        copy.wait()
    edge = dot(halo_ref[...], wi_ref[:, :width]).astype(BF16).astype(F32)
    north, south = row > 0, row < n - 1
    lwest, least = col > 0, col < n - 1

    def seen(slot, ok, first=0, count=tc):
        return jnp.where(ok, edge[slot * tc + first : slot * tc + first + count], 0.0)

    n_all, s_all = seen(0, north), seen(1, south)
    w_all, e_all = seen(2, lwest), seen(3, least)
    nw, ne = seen(4, north & lwest, tc - 8, 8), seen(5, north & least, 0, 8)
    sw, se = seen(6, south & lwest, tc - 8, 8), seen(7, south & least, 0, 8)
    for k in range(groups):
        pad_ref[k, 0, 8 : 8 + tc, :] = n_all[:, cols(k)]
        pad_ref[k, tr + 1, 8 : 8 + tc, :] = s_all[:, cols(k)]
        pad_ref[k, 0, 0:8, :] = nw[:, cols(k)]
        pad_ref[k, 0, 8 + tc : 16 + tc, :] = ne[:, cols(k)]
        pad_ref[k, tr + 1, 0:8, :] = sw[:, cols(k)]
        pad_ref[k, tr + 1, 8 + tc : 16 + tc, :] = se[:, cols(k)]
        for r in range(tr):
            pad_ref[k, 1 + r, 7:8, :] = w_all[r : r + 1, cols(k)]
            pad_ref[k, 1 + r, 8 + tc : 9 + tc, :] = e_all[r : r + 1, cols(k)]
    bias = cb_ref[...].reshape(1, width)

    def convolve(r, _):
        for k in range(groups):
            total = jnp.broadcast_to(bias[:, cols(k)], (tc, LANES))
            for a in range(3):
                for b in range(3):
                    total = total + pad_ref[k, r + a, 7 + b : 7 + b + tc, :] * cw_ref[a, b : b + 1, cols(k)]
            done = silu(total).astype(BF16)
            act_ref[r, :, cols(k)] = done
            actf_ref[k, tile(r), :] = done.astype(F32)
        return 0

    lax.fori_loop(0, tr, convolve, 0)

    def token_copy(axis, step, peer, owner):
        src = (act_ref if axis == 0 else actt_ref).at[peer]
        return remote(
            src, line_ref.at[axis, tile(owner)], ts_sem.at[axis, step], tr_sem.at[axis, owner], *across(axis, peer)
        )

    def token_arrival(axis, step, peer):
        remote(
            act_ref.at[0], line_ref.at[axis, tile(peer)], ts_sem.at[axis, step], tr_sem.at[axis, peer],
            *across(axis, peer),
        ).wait_recv()

    every(0, lambda step, peer: token_copy(0, step, peer, col).start())

    def flip(j, _):
        for k in range(groups):
            actt_ref[j, :, cols(k)] = actf_ref[k, pl.ds(j, tr, stride=tc), :].astype(BF16)
        return 0

    lax.fori_loop(0, tc, flip, 0)
    every(1, lambda step, peer: token_copy(1, step, peer, row).start())
    line_ref[0, tile(col), :] = act_ref[col]
    line_ref[1, tile(row), :] = actt_ref[row]

    def gates(i, _):
        at = pl.ds(pl.multiple_of(i * step, step), step)
        gate = dot(nb_ref[at, :], wi_ref[:, width:]).astype(BF16).astype(F32)
        gate_ref[at, :] = silu(gate)
        return 0

    lax.fori_loop(0, tokens // step, gates, 0)
    fetch[4].wait()

    def rates(d, _):
        for k in range(groups):
            dec_ref[d, k] = jnp.exp(dl_ref[d, :, cols(k)]) * -LOG2E
        return 0

    lax.fori_loop(0, dl_ref.shape[0], rates, 0)
    for i in (2, 3, 5):
        fetch[i].wait()

    span = 16
    blocks = length // span
    held = (ha_ref, hb_ref)
    kk, cc = iota((parts, span * states), 0), iota((parts, span * states), 1)
    lane = iota((states, LANES), 1)

    def scan_line(line, _):
        every(line, lambda step, peer: token_arrival(line, step, peer))

        def prepare(d, _):
            which = line * 2 + d
            repeat = (kk == rank + states + lax.rem(cc, states)).astype(BF16)
            mask = lax.rem(iota((length, span * states), 0), span) == iota((length, span * states), 1) // states
            u = line_ref[line]
            p = dot_nt(u, pw_ref[which])
            high = p.astype(BF16)
            ph_ref[d] = high
            pl_ref[d] = (p - high.astype(F32)).astype(BF16)
            mc_ref[d] = jnp.where(mask, dot(high, repeat), 0.0).astype(BF16)
            enter = dot_nt(pw_ref[which, rank : rank + states, :], u)
            ones = jnp.ones((LANES, LANES), BF16)
            for h in range(length // LANES):
                for g in range(0, LANES, span):
                    spread = [jnp.where(lane == g + i, enter[:, cols(h)], 0.0) for i in range(span)]
                    at = (h * LANES + g) * states
                    bb_ref[d, at : at + span * states, :] = dot(jnp.concatenate(spread, axis=0).astype(BF16), ones)
            weight = sw_ref[which]
            swh = weight.astype(BF16)
            swl = (weight - swh.astype(F32)).astype(BF16)
            shift = sb_ref[pl.ds(which, 1), :]

            def step_size(i, _):
                at = pl.ds(pl.multiple_of(i * 32, 32), 32)
                a = ph_ref[d, at, :rank]
                s = softplus(dot(a, swh) + (dot(a, swl) + dot(pl_ref[d, at, :rank], swh)) + shift)
                du = s * line_ref[line, at, :].astype(F32)
                for k in range(groups):
                    s_ref[d, k, at, :] = s[:, cols(k)]
                    du_ref[d, k, at, :] = du[:, cols(k)]
                return 0

            lax.fori_loop(0, length // 32, step_size, 0)
            return 0

        lax.fori_loop(0, 2, prepare, 0)
        skip = sk_ref[pl.ds(line * 2, 1), :] + sk_ref[pl.ds(line * 2 + 1, 1), :]

        def begin(i, _):
            at = pl.ds(pl.multiple_of(i * 32, 32), 32)
            v = line_ref[line, at, :].astype(F32) * skip
            for c in range(chunks):
                acc_ref[c, at, :] = v[:, c * chunk : (c + 1) * chunk]
            return 0

        lax.fori_loop(0, length // 32, begin, 0)

        def scan_chunk(c, _):
            g0 = c * per
            dec = [
                [[dec_ref[line * 2 + d, g0 + k, 8 * v : 8 * v + 8, :] for v in range(2)] for k in range(per)]
                for d in range(2)
            ]

            def leave(slot, i, d):
                b = pl.multiple_of((i if d == 0 else blocks - 1 - i) * span, span)
                states_now = jnp.concatenate([held[slot][d, k] for k in range(per)], axis=1)
                acc_ref[c, pl.ds(b, span), :] += dot(mc_ref[d, pl.ds(b, span), :], states_now)

            def advance(slot, i, h):
                base = (i * span, (blocks - 1 - i) * span)
                for j in range(span):
                    for d in range(2):
                        jj = j if d == 0 else span - 1 - j
                        t = base[d] + jj
                        enter = [bb_ref[d, pl.ds(pl.multiple_of(t * states + 8 * v, 8), 8), :] for v in range(2)]
                        for k in range(per):
                            s = s_ref[d, g0 + k, pl.ds(t, 8, stride=0), :]
                            du = du_ref[d, g0 + k, pl.ds(t, 8, stride=0), :]
                            now = [jnp.exp2(s * dec[d][k][v]) * h[d][k][v] + du * enter[v] for v in range(2)]
                            h[d][k] = now
                            held[slot][d, k, jj * states : (jj + 1) * states, :] = jnp.concatenate(
                                now, axis=0
                            ).astype(BF16)
                return h

            def body(i, h):
                h = [[list(v) for v in part] for part in h]
                for d in range(2):
                    leave(1, jnp.maximum(2 * i - 1, 0), d)
                h = advance(0, 2 * i, h)
                for d in range(2):
                    leave(0, 2 * i, d)
                h = advance(1, 2 * i + 1, h)
                return tuple(tuple(tuple(v) for v in part) for part in h)

            hb_ref[...] = jnp.zeros_like(hb_ref)
            zero = jnp.zeros((8, LANES), F32)
            lax.fori_loop(0, blocks // 2, body, tuple(tuple((zero, zero) for _ in range(per)) for _ in range(2)))
            for d in range(2):
                leave(1, blocks - 1, d)
            y_ref[line, c] = acc_ref[c].astype(BF16)
            me = mine(line)
            every(line, lambda step, peer: result_copy(line, c, step, peer, me).start())
            land_ref[line, c, me] = y_ref[line, c, tile(me), :]
            return 0

        lax.fori_loop(0, chunks, scan_chunk, 0)
        return 0

    def result_copy(axis, c, step, peer, owner):
        return remote(
            y_ref.at[axis, c, tile(peer)], land_ref.at[axis, c, owner], ys_sem.at[axis, c, step],
            yr_sem.at[axis, c, owner], *across(axis, peer),
        )

    lax.fori_loop(0, 2, scan_line, 0)
    for axis in range(2):
        every(axis, lambda step, peer: token_copy(axis, step, peer, mine(axis)).wait_send())

    def arrive(axis, c, _):
        every(axis, lambda step, peer: result_copy(axis, c, step, peer, peer).wait_recv())
        return 0

    lax.fori_loop(0, chunks, lambda c, _: arrive(0, c, _), 0)
    for c in range(chunks):
        arrive(1, c, 0)

        def widen(j, _):
            for k in range(per):
                cf_ref[c * per + k, tile(j), :] = land_ref[1, c, j, :, cols(k)].astype(F32)
            return 0

        lax.fori_loop(0, tc, widen, 0)

    def finish(r, _):
        other = jnp.concatenate([cf_ref[k, pl.ds(r, tc, stride=tr), :] for k in range(groups)], axis=1)
        v = jnp.concatenate([land_ref[0, c, r] for c in range(chunks)], axis=1).astype(F32) + other
        v = v - jnp.mean(v, axis=-1, keepdims=True)
        v = v * lax.rsqrt(jnp.mean(v * v, axis=-1, keepdims=True) + 1e-05) * og_ref[...].reshape(1, width)
        go_ref[tile(r), :] = (v * gate_ref[tile(r), :]).astype(BF16)
        return 0

    lax.fori_loop(0, tr, finish, 0)
    out_ref[...] = dot(go_ref[...], wo_ref[...]).astype(BF16).reshape(out_ref.shape)

    def sent(c, _):
        for axis in range(2):
            every(axis, lambda step, peer: result_copy(axis, c, step, peer, mine(axis)).wait_send())
        return 0

    lax.fori_loop(0, chunks, sent, 0)


def local(
    n, features, norm_gain, in_weight, conv_weight, conv_bias, proj_weight, step_weight, step_bias,
    decay_log, skip_gain, out_gain, out_weight,
):
    tr, tc, channels = features.shape
    width = out_weight.shape[0]
    tokens = tr * tc
    groups = width // LANES
    length = tc * n
    dma = pltpu.SemaphoreType.DMA
    pw = jnp.swapaxes(proj_weight, 1, 2)
    dl = jnp.swapaxes(decay_log, 1, 2)
    parts, states = pw.shape[1], dl.shape[1]
    span, per = 16, 2
    chunks = groups // per
    hbm = pl.BlockSpec(memory_space=pl.ANY)
    like = lambda a: pltpu.VMEM(a.shape, a.dtype)
    return pl.pallas_call(
        functools.partial(block_kernel, n, per),
        out_shape=jax.ShapeDtypeStruct(features.shape, BF16),
        in_specs=[hbm, VMEM, hbm, VMEM, VMEM, hbm, hbm, VMEM, hbm, VMEM, VMEM, hbm],
        out_specs=VMEM,
        scratch_shapes=[
            like(features), like(in_weight), like(pw), like(step_weight), like(dl), like(out_weight),
            pltpu.VMEM((tokens, channels), BF16),
            pltpu.VMEM((channels // LANES, tokens, LANES), F32),
            pltpu.VMEM((2, tr, channels), BF16),
            pltpu.VMEM((8 * tc, channels), BF16),
            pltpu.VMEM((groups, tr + 2, tc + 16, LANES), F32),
            pltpu.VMEM((tr, tc, width), BF16),
            pltpu.VMEM((tc, tr, width), BF16),
            pltpu.VMEM((groups, tokens, LANES), F32),
            pltpu.VMEM((2, length, width), BF16),
            pltpu.VMEM((tokens, width), F32),
            pltpu.VMEM((2, length, parts), BF16),
            pltpu.VMEM((2, length, parts), BF16),
            pltpu.VMEM((2, groups, length, LANES), F32),
            pltpu.VMEM((2, groups, length, LANES), F32),
            pltpu.VMEM((2, length * states, LANES), F32),
            pltpu.VMEM((2, length, span * states), BF16),
            pltpu.VMEM((dl.shape[0], groups, states, LANES), F32),
            pltpu.VMEM((2, per, span * states, LANES), BF16),
            pltpu.VMEM((2, per, span * states, LANES), BF16),
            pltpu.VMEM((chunks, length, per * LANES), F32),
            pltpu.VMEM((2, chunks, length, per * LANES), BF16),
            pltpu.VMEM((2, chunks, n, tc, per * LANES), BF16),
            pltpu.VMEM((groups, tokens, LANES), F32),
            pltpu.VMEM((tokens, width), BF16),
            dma((6,)), dma((8,)), dma((8,)), dma((2, n)), dma((2, n)), dma((2, chunks, n)), dma((2, chunks, n)),
        ],
        compiler_params=pltpu.CompilerParams(collective_id=0, has_side_effects=True, vmem_limit_bytes=60 << 20),
    )(
        features, norm_gain, in_weight, conv_weight, conv_bias, pw, step_weight, step_bias, dl, skip_gain,
        out_gain, out_weight,
    )


def solution(mesh):
    n = mesh.shape["row"]
    assert mesh.shape["col"] == n
    in_specs = (P("row", "col", None), P(), P(), P(), P(), P(), P(), P(), P(), P(), P(), P())
    return jax.shard_map(
        functools.partial(local, n), mesh=mesh, in_specs=in_specs, out_specs=P("row", "col", None), check_vma=False
    )
```

```python
import functools

import jax
import jax.numpy as jnp
from jax import lax
from jax.experimental import pallas as pl
from jax.experimental.pallas import tpu as pltpu
from jax.sharding import PartitionSpec as P

F32 = jnp.float32
BF16 = jnp.bfloat16
MESH = pl.DeviceIdType.MESH
NT = (((1,), (1,)), ((), ()))
LANES = 128
LOG2E = 1.4426950408889634
PIECE = 2
VMEM = pl.BlockSpec(memory_space=pltpu.VMEM)


def dot(a, b):
    return jnp.dot(a, b, preferred_element_type=F32)


def dot_nt(a, b):
    return lax.dot_general(a, b, NT, preferred_element_type=F32)


def softplus(z):
    w = jnp.exp2(jnp.abs(z) * -LOG2E)
    small = w * (1.0 - w * (0.5 - w * (1.0 / 3.0)))
    return jnp.maximum(z, 0.0) + jnp.where(w < 0.01, small, jnp.log(1.0 + w))


def silu(v):
    return v / (1.0 + jnp.exp(-v))


def iota(shape, dim):
    return lax.broadcasted_iota(jnp.int32, shape, dim)


def cols(k):
    return slice(k * LANES, (k + 1) * LANES)


def place():
    return lax.axis_index("row"), lax.axis_index("col")


def greet(nr, nc):
    row, col = place()
    sem = pltpu.get_barrier_semaphore()

    def signal(r, c):
        pl.semaphore_signal(sem, inc=1, device_id={"row": r, "col": c}, device_id_type=MESH)

    def along_col(k, _):
        signal(row, lax.rem(col + k, nc))
        return 0

    def along_row(k, _):
        signal(lax.rem(row + k, nr), col)
        return 0

    lax.fori_loop(1, nc, along_col, 0)
    lax.fori_loop(1, nr, along_row, 0)
    for dr in (1, nr - 1):
        for dc in (1, nc - 1):
            signal(lax.rem(row + dr, nr), lax.rem(col + dc, nc))
    return lambda: pl.semaphore_wait(sem, nr + nc + 2)


def remote(src, dst, send_sem, recv_sem, r, c):
    return pltpu.make_async_remote_copy(
        src_ref=src, dst_ref=dst, send_sem=send_sem, recv_sem=recv_sem,
        device_id={"row": r, "col": c}, device_id_type=MESH,
    )


def block_kernel(
    n, per, x_hbm, gain_ref, wi_hbm, cw_ref, cb_ref, pw_hbm, sw_hbm, sb_ref, dl_hbm, sk_ref, og_ref, wo_hbm, out_ref,
    x_ref, wi_ref, pw_ref, sw_ref, dl_ref, wo_ref,
    nb_ref, nf_ref, strip_ref, halo_ref, pad_ref, act_ref, actt_ref, actf_ref, line_ref, gate_ref,
    s_ref, du_ref, bb_ref, mc_ref, dec_ref, ha_ref, hb_ref, acc_ref, y_ref, land_ref, cf_ref, go_ref,
    own_sem, hs_sem, hr_sem, ts_sem, tr_sem, ys_sem, yr_sem,
):
    tr, tc, channels = x_ref.shape
    width = cb_ref.shape[-1]
    tokens = tr * tc
    groups = width // LANES
    chunks = groups // per
    chunk = per * LANES
    length = line_ref.shape[1]
    rank, states = sw_ref.shape[1], dl_ref.shape[1]
    row, col = place()
    fetch = [
        pltpu.make_async_copy(src, dst, own_sem.at[i])
        for i, (src, dst) in enumerate(
            ((x_hbm, x_ref), (wi_hbm, wi_ref), (pw_hbm, pw_ref), (sw_hbm, sw_ref), (dl_hbm, dl_ref), (wo_hbm, wo_ref))
        )
    ]
    for copy in fetch:
        copy.start()
    greeted = greet(n, n)

    def mine(axis):
        return col + axis * (row - col)

    def across(axis, peer):
        return row + axis * (peer - row), peer + axis * (col - peer)

    def every(axis, one):
        me = mine(axis)

        def body(step, _):
            one(step, lax.rem(me + step, n))
            return 0

        lax.fori_loop(1, n, body, 0)

    def tile(i):
        return pl.ds(pl.multiple_of(i * tc, tc), tc)

    step = 4 * tc
    fetch[0].wait()

    def norm(i, _):
        v = x_ref[pl.ds(i * 4, 4)].reshape(step, channels).astype(F32)
        v = v - jnp.mean(v, axis=-1, keepdims=True)
        v = v * lax.rsqrt(jnp.mean(v * v, axis=-1, keepdims=True) + 1e-05) * gain_ref[...].reshape(1, channels)
        at = pl.ds(pl.multiple_of(i * step, step), step)
        nb_ref[at, :] = v.astype(BF16)
        for k in range(channels // LANES):
            nf_ref[k, at, :] = v[:, cols(k)]
        return 0

    lax.fori_loop(0, tokens // step, norm, 0)
    for k in range(channels // LANES):
        strip_ref[0, :, cols(k)] = nf_ref[k, pl.ds(0, tr, stride=tc), :].astype(BF16)
        strip_ref[1, :, cols(k)] = nf_ref[k, pl.ds(tc - 1, tr, stride=tc), :].astype(BF16)
    top, bottom = nb_ref.at[pl.ds(0, tc)], nb_ref.at[pl.ds(tokens - tc, tc)]
    left, right = strip_ref.at[0], strip_ref.at[1]
    up, down = lax.rem(row + n - 1, n), lax.rem(row + 1, n)
    west, east = lax.rem(col + n - 1, n), lax.rem(col + 1, n)
    fetch[1].wait()

    def project(i, _):
        at = pl.ds(pl.multiple_of(i * step, step), step)
        inner = dot(nb_ref[at, :], wi_ref[:, :width]).astype(BF16).astype(F32)
        for k in range(groups):
            pad_ref[k, pl.ds(1 + i * 4, 4), 8 : 8 + tc, :] = inner[:, cols(k)].reshape(4, tc, LANES)
        return 0

    lax.fori_loop(0, tokens // step, project, 0)

    def gates(i, _):
        at = pl.ds(pl.multiple_of(i * step, step), step)
        gate = dot(nb_ref[at, :], wi_ref[:, width:]).astype(BF16).astype(F32)
        gate_ref[at, :] = silu(gate)
        return 0

    lax.fori_loop(0, tokens // step, gates, 0)
    for i in (2, 3, 4, 5):
        fetch[i].wait()

    def rates(d, _):
        for k in range(groups):
            dec_ref[d, k] = jnp.exp(dl_ref[d, :, cols(k)]) * -LOG2E
        return 0

    lax.fori_loop(0, dl_ref.shape[0], rates, 0)
    greeted()
    plan = (
        (bottom, down, col), (top, up, col), (right, row, east), (left, row, west),
        (bottom, down, east), (bottom, down, west), (top, up, east), (top, up, west),
    )
    halos = [
        remote(src, halo_ref.at[pl.ds(slot * tc, tc)], hs_sem.at[slot], hr_sem.at[slot], r, c)
        for slot, (src, r, c) in enumerate(plan)
    ]
    for copy in halos:
        copy.start()
    for copy in halos:
        copy.wait()
    edge = dot(halo_ref[...], wi_ref[:, :width]).astype(BF16).astype(F32)
    north, south = row > 0, row < n - 1
    lwest, least = col > 0, col < n - 1

    def seen(slot, ok, first=0, count=tc):
        return jnp.where(ok, edge[slot * tc + first : slot * tc + first + count], 0.0)

    n_all, s_all = seen(0, north), seen(1, south)
    w_all, e_all = seen(2, lwest), seen(3, least)
    nw, ne = seen(4, north & lwest, tc - 8, 8), seen(5, north & least, 0, 8)
    sw, se = seen(6, south & lwest, tc - 8, 8), seen(7, south & least, 0, 8)
    for k in range(groups):
        pad_ref[k, 0, 8 : 8 + tc, :] = n_all[:, cols(k)]
        pad_ref[k, tr + 1, 8 : 8 + tc, :] = s_all[:, cols(k)]
        pad_ref[k, 0, 0:8, :] = nw[:, cols(k)]
        pad_ref[k, 0, 8 + tc : 16 + tc, :] = ne[:, cols(k)]
        pad_ref[k, tr + 1, 0:8, :] = sw[:, cols(k)]
        pad_ref[k, tr + 1, 8 + tc : 16 + tc, :] = se[:, cols(k)]
        for r in range(tr):
            pad_ref[k, 1 + r, 7:8, :] = w_all[r : r + 1, cols(k)]
            pad_ref[k, 1 + r, 8 + tc : 9 + tc, :] = e_all[r : r + 1, cols(k)]
    bias = cb_ref[...].reshape(1, width)

    def convolve(r, _):
        for k in range(groups):
            total = jnp.broadcast_to(bias[:, cols(k)], (tc, LANES))
            for a in range(3):
                for b in range(3):
                    total = total + pad_ref[k, r + a, 7 + b : 7 + b + tc, :] * cw_ref[a, b : b + 1, cols(k)]
            done = silu(total).astype(BF16)
            act_ref[r, :, cols(k)] = done
            actf_ref[k, tile(r), :] = done.astype(F32)
        return 0

    lax.fori_loop(0, tr, convolve, 0)

    def token_copy(axis, step, peer, owner):
        src = (act_ref if axis == 0 else actt_ref).at[peer]
        return remote(
            src, line_ref.at[axis, tile(owner)], ts_sem.at[axis, step], tr_sem.at[axis, owner], *across(axis, peer)
        )

    def token_arrival(axis, step, peer):
        remote(
            act_ref.at[0], line_ref.at[axis, tile(peer)], ts_sem.at[axis, step], tr_sem.at[axis, peer],
            *across(axis, peer),
        ).wait_recv()

    every(0, lambda step, peer: token_copy(0, step, peer, col).start())

    def flip(j, _):
        for k in range(groups):
            actt_ref[j, :, cols(k)] = actf_ref[k, pl.ds(j, tr, stride=tc), :].astype(BF16)
        return 0

    lax.fori_loop(0, tc, flip, 0)
    line_ref[0, tile(col), :] = act_ref[col]
    line_ref[1, tile(row), :] = actt_ref[row]

    span = 16
    blocks = length // span
    held = (ha_ref, hb_ref)
    kk, cc = iota((3 * rank + states, span * states), 0), iota((3 * rank + states, span * states), 1)
    lane = iota((states, LANES), 1)

    def scan_line(line):

        def prepare(d, _):
            which = line * 2 + d
            repeat = (kk == 3 * rank + lax.rem(cc, states)).astype(BF16)
            mask = lax.rem(iota((length, span * states), 0), span) == iota((length, span * states), 1) // states
            u = line_ref[line]
            to_rank = pw_ref[which, :rank, :]
            p = dot_nt(u, jnp.concatenate([to_rank] * 3 + [pw_ref[which, rank + states :, :]], axis=0))
            high = p.astype(BF16)
            low = p - high.astype(F32)
            stacked = jnp.where(iota(p.shape, 1) < 2 * rank, high.astype(F32), low).astype(BF16)[:, : 3 * rank]
            mc_ref[d] = jnp.where(mask, dot(high, repeat), 0.0).astype(BF16)
            weight = sw_ref[which]
            swh = weight.astype(BF16)
            swl = (weight - swh.astype(F32)).astype(BF16)
            weights = jnp.concatenate([swh, swl, swh], axis=0)
            shift = sb_ref[pl.ds(which, 1), :]
            wide = PIECE * LANES
            for g in range(0, groups, PIECE):
                at = slice(g * LANES, g * LANES + wide)
                s = softplus(dot(stacked, weights[:, at]) + shift[:, at])
                du = s * line_ref[line, :, at].astype(F32)
                for k in range(PIECE):
                    s_ref[d, g + k] = s[:, cols(k)]
                    du_ref[d, g + k] = du[:, cols(k)]
            enter = dot_nt(pw_ref[which, rank : rank + states, :], u)
            ones = jnp.ones((LANES, LANES), BF16)
            for h in range(length // LANES):
                for g in range(0, LANES, span):
                    spread = [jnp.where(lane == g + i, enter[:, cols(h)], 0.0) for i in range(span)]
                    at = (h * LANES + g) * states
                    bb_ref[d, at : at + span * states, :] = dot(jnp.concatenate(spread, axis=0).astype(BF16), ones)
            return 0

        lax.fori_loop(0, 2, prepare, 0)
        skip = sk_ref[pl.ds(line * 2, 1), :] + sk_ref[pl.ds(line * 2 + 1, 1), :]

        def begin(i, _):
            at = pl.ds(pl.multiple_of(i * 32, 32), 32)
            v = line_ref[line, at, :].astype(F32) * skip
            for c in range(chunks):
                acc_ref[c, at, :] = v[:, c * chunk : (c + 1) * chunk]
            return 0

        lax.fori_loop(0, length // 32, begin, 0)

        def scan_chunk(c, _):
            g0 = c * per
            dec = [
                [[dec_ref[line * 2 + d, g0 + k, 8 * v : 8 * v + 8, :] for v in range(2)] for k in range(per)]
                for d in range(2)
            ]

            def leave(slot, i, d):
                b = pl.multiple_of((i if d == 0 else blocks - 1 - i) * span, span)
                states_now = jnp.concatenate([held[slot][d, k] for k in range(per)], axis=1)
                acc_ref[c, pl.ds(b, span), :] += dot(mc_ref[d, pl.ds(b, span), :], states_now)

            def advance(slot, i, h):
                base = (i * span, (blocks - 1 - i) * span)
                for j in range(span):
                    for d in range(2):
                        jj = j if d == 0 else span - 1 - j
                        t = base[d] + jj
                        enter = [bb_ref[d, pl.ds(pl.multiple_of(t * states + 8 * v, 8), 8), :] for v in range(2)]
                        for k in range(per):
                            s = s_ref[d, g0 + k, pl.ds(t, 8, stride=0), :]
                            du = du_ref[d, g0 + k, pl.ds(t, 8, stride=0), :]
                            now = [jnp.exp2(s * dec[d][k][v]) * h[d][k][v] + du * enter[v] for v in range(2)]
                            h[d][k] = now
                            held[slot][d, k, jj * states : (jj + 1) * states, :] = jnp.concatenate(
                                now, axis=0
                            ).astype(BF16)
                return h

            def body(i, h):
                h = [[list(v) for v in part] for part in h]
                for d in range(2):
                    leave(1, jnp.maximum(2 * i - 1, 0), d)
                h = advance(0, 2 * i, h)
                for d in range(2):
                    leave(0, 2 * i, d)
                h = advance(1, 2 * i + 1, h)
                return tuple(tuple(tuple(v) for v in part) for part in h)

            hb_ref[...] = jnp.zeros_like(hb_ref)
            zero = jnp.zeros((8, LANES), F32)
            lax.fori_loop(0, blocks // 2, body, tuple(tuple((zero, zero) for _ in range(per)) for _ in range(2)))
            for d in range(2):
                leave(1, blocks - 1, d)
            y_ref[line, c] = acc_ref[c].astype(BF16)
            me = mine(line)
            every(line, lambda step, peer: result_copy(line, c, step, peer, me).start())
            land_ref[line, c, me] = y_ref[line, c, tile(me), :]
            return 0

        lax.fori_loop(0, chunks, scan_chunk, 0)

    def result_copy(axis, c, step, peer, owner):
        return remote(
            y_ref.at[axis, c, tile(peer)], land_ref.at[axis, c, owner], ys_sem.at[axis, c, step],
            yr_sem.at[axis, c, owner], *across(axis, peer),
        )

    every(0, lambda step, peer: token_arrival(0, step, peer))
    every(1, lambda step, peer: token_copy(1, step, peer, row).start())
    scan_line(0)
    every(1, lambda step, peer: token_arrival(1, step, peer))
    scan_line(1)
    for axis in range(2):
        every(axis, lambda step, peer: token_copy(axis, step, peer, mine(axis)).wait_send())

    def arrive(axis, c, _):
        every(axis, lambda step, peer: result_copy(axis, c, step, peer, peer).wait_recv())
        return 0

    lax.fori_loop(0, chunks, lambda c, _: arrive(0, c, _), 0)
    for c in range(chunks):
        arrive(1, c, 0)

        def widen(j, _):
            for k in range(per):
                cf_ref[c * per + k, tile(j), :] = land_ref[1, c, j, :, cols(k)].astype(F32)
            return 0

        lax.fori_loop(0, tc, widen, 0)

    def finish(r, _):
        other = jnp.concatenate([cf_ref[k, pl.ds(r, tc, stride=tr), :] for k in range(groups)], axis=1)
        v = jnp.concatenate([land_ref[0, c, r] for c in range(chunks)], axis=1).astype(F32) + other
        v = v - jnp.mean(v, axis=-1, keepdims=True)
        v = v * lax.rsqrt(jnp.mean(v * v, axis=-1, keepdims=True) + 1e-05) * og_ref[...].reshape(1, width)
        go_ref[tile(r), :] = (v * gate_ref[tile(r), :]).astype(BF16)
        return 0

    lax.fori_loop(0, tr, finish, 0)
    out_ref[...] = dot(go_ref[...], wo_ref[...]).astype(BF16).reshape(out_ref.shape)

    def sent(c, _):
        for axis in range(2):
            every(axis, lambda step, peer: result_copy(axis, c, step, peer, mine(axis)).wait_send())
        return 0

    lax.fori_loop(0, chunks, sent, 0)


def local(
    n, features, norm_gain, in_weight, conv_weight, conv_bias, proj_weight, step_weight, step_bias,
    decay_log, skip_gain, out_gain, out_weight,
):
    tr, tc, channels = features.shape
    width = out_weight.shape[0]
    tokens = tr * tc
    groups = width // LANES
    length = tc * n
    dma = pltpu.SemaphoreType.DMA
    pw = jnp.swapaxes(proj_weight, 1, 2)
    dl = jnp.swapaxes(decay_log, 1, 2)
    states = dl.shape[1]
    span, per = 16, 3
    chunks = groups // per
    hbm = pl.BlockSpec(memory_space=pl.ANY)
    like = lambda a: pltpu.VMEM(a.shape, a.dtype)
    return pl.pallas_call(
        functools.partial(block_kernel, n, per),
        out_shape=jax.ShapeDtypeStruct(features.shape, BF16),
        in_specs=[hbm, VMEM, hbm, VMEM, VMEM, hbm, hbm, VMEM, hbm, VMEM, VMEM, hbm],
        out_specs=VMEM,
        scratch_shapes=[
            like(features), like(in_weight), like(pw), like(step_weight), like(dl), like(out_weight),
            pltpu.VMEM((tokens, channels), BF16),
            pltpu.VMEM((channels // LANES, tokens, LANES), F32),
            pltpu.VMEM((2, tr, channels), BF16),
            pltpu.VMEM((8 * tc, channels), BF16),
            pltpu.VMEM((groups, tr + 2, tc + 16, LANES), F32),
            pltpu.VMEM((tr, tc, width), BF16),
            pltpu.VMEM((tc, tr, width), BF16),
            pltpu.VMEM((groups, tokens, LANES), F32),
            pltpu.VMEM((2, length, width), BF16),
            pltpu.VMEM((tokens, width), F32),
            pltpu.VMEM((2, groups, length, LANES), F32),
            pltpu.VMEM((2, groups, length, LANES), F32),
            pltpu.VMEM((2, length * states, LANES), F32),
            pltpu.VMEM((2, length, span * states), BF16),
            pltpu.VMEM((dl.shape[0], groups, states, LANES), F32),
            pltpu.VMEM((2, per, span * states, LANES), BF16),
            pltpu.VMEM((2, per, span * states, LANES), BF16),
            pltpu.VMEM((chunks, length, per * LANES), F32),
            pltpu.VMEM((2, chunks, length, per * LANES), BF16),
            pltpu.VMEM((2, chunks, n, tc, per * LANES), BF16),
            pltpu.VMEM((groups, tokens, LANES), F32),
            pltpu.VMEM((tokens, width), BF16),
            dma((6,)), dma((8,)), dma((8,)), dma((2, n)), dma((2, n)), dma((2, chunks, n)), dma((2, chunks, n)),
        ],
        compiler_params=pltpu.CompilerParams(collective_id=0, has_side_effects=True, vmem_limit_bytes=60 << 20),
    )(
        features, norm_gain, in_weight, conv_weight, conv_bias, pw, step_weight, step_bias, dl, skip_gain,
        out_gain, out_weight,
    )


def solution(mesh):
    n = mesh.shape["row"]
    assert mesh.shape["col"] == n
    in_specs = (P("row", "col", None), P(), P(), P(), P(), P(), P(), P(), P(), P(), P(), P())
    return jax.shard_map(
        functools.partial(local, n), mesh=mesh, in_specs=in_specs, out_specs=P("row", "col", None), check_vma=False
    )
```

```python
import functools

import jax
import jax.numpy as jnp
from jax import lax
from jax.experimental import pallas as pl
from jax.experimental.pallas import tpu as pltpu
from jax.sharding import PartitionSpec as P

F32 = jnp.float32
BF16 = jnp.bfloat16
MESH = pl.DeviceIdType.MESH
NT = (((1,), (1,)), ((), ()))
LANES = 128
LOG2E = 1.4426950408889634
PIECE = 2
PER = (3, 2)
VMEM = pl.BlockSpec(memory_space=pltpu.VMEM)


def dot(a, b):
    return jnp.dot(a, b, preferred_element_type=F32)


def dot_nt(a, b):
    return lax.dot_general(a, b, NT, preferred_element_type=F32)


def softplus(z):
    w = jnp.exp2(jnp.abs(z) * -LOG2E)
    small = w * (1.0 - w * (0.5 - w * (1.0 / 3.0)))
    return jnp.maximum(z, 0.0) + jnp.where(w < 0.01, small, jnp.log(1.0 + w))


def silu(v):
    return v / (1.0 + jnp.exp(-v))


def iota(shape, dim):
    return lax.broadcasted_iota(jnp.int32, shape, dim)


def cols(k):
    return slice(k * LANES, (k + 1) * LANES)


def place():
    return lax.axis_index("row"), lax.axis_index("col")


def greet(nr, nc):
    row, col = place()
    sem = pltpu.get_barrier_semaphore()

    def signal(r, c):
        pl.semaphore_signal(sem, inc=1, device_id={"row": r, "col": c}, device_id_type=MESH)

    def along_col(k, _):
        signal(row, lax.rem(col + k, nc))
        return 0

    def along_row(k, _):
        signal(lax.rem(row + k, nr), col)
        return 0

    lax.fori_loop(1, nc, along_col, 0)
    lax.fori_loop(1, nr, along_row, 0)
    for dr in (1, nr - 1):
        for dc in (1, nc - 1):
            signal(lax.rem(row + dr, nr), lax.rem(col + dc, nc))
    return lambda: pl.semaphore_wait(sem, nr + nc + 2)


def remote(src, dst, send_sem, recv_sem, r, c):
    return pltpu.make_async_remote_copy(
        src_ref=src, dst_ref=dst, send_sem=send_sem, recv_sem=recv_sem,
        device_id={"row": r, "col": c}, device_id_type=MESH,
    )


def block_kernel(
    n, x_hbm, gain_hbm, wi_hbm, cw_hbm, cb_hbm, pw_hbm, sw_hbm, sb_hbm, dl_hbm, sk_hbm, og_hbm, wo_hbm, out_ref,
    x_ref, gain_ref, wi_ref, cw_ref, cb_ref, pw_ref, sw_ref, sb_ref, dl_ref, sk_ref, og_ref, wo_ref,
    nb_ref, nf_ref, strip_ref, halo_ref, pad_ref, act_ref, actt_ref, actf_ref, line_ref, gate_ref,
    s_ref, du_ref, bb_ref, mc_ref, dec_ref, ha_ref, hb_ref, acc_ref, y_ref, land_ref, cf_ref, go_ref,
    st_ref, sl_ref, own_sem, hs_sem, hr_sem, ts_sem, tr_sem, ys_sem, yr_sem, ss_sem, sr_sem,
):
    tr, tc, channels = x_ref.shape
    width = cb_ref.shape[-1]
    tokens = tr * tc
    groups = width // LANES
    length = line_ref.shape[1]
    rank, states = sw_ref.shape[1], dl_ref.shape[1]
    row, col = place()
    there = (x_hbm, gain_hbm, wi_hbm, cw_hbm, cb_hbm, pw_hbm, sw_hbm, sb_hbm, dl_hbm, sk_hbm, og_hbm, wo_hbm)
    here = (x_ref, gain_ref, wi_ref, cw_ref, cb_ref, pw_ref, sw_ref, sb_ref, dl_ref, sk_ref, og_ref, wo_ref)
    fetch = [pltpu.make_async_copy(src, dst, own_sem.at[i]) for i, (src, dst) in enumerate(zip(there, here))]
    for copy in fetch:
        copy.start()
    greeted = greet(n, n)

    half = n // 2
    side, seat = col // half, lax.rem(col, half)

    def others(one):
        def body(step, _):
            one(step, lax.rem(row + step, n))
            return 0

        lax.fori_loop(1, n, body, 0)

    def mates(one):
        def body(step, _):
            r = lax.rem(2 * seat + step, n)
            one(r, r // 2, lax.rem(r, 2))
            return 0

        lax.fori_loop(2, n, body, 0)

    def tile(i):
        return pl.ds(pl.multiple_of(i * tc, tc), tc)

    step = 4 * tc
    fetch[0].wait()
    fetch[1].wait()

    def norm(i, _):
        v = x_ref[pl.ds(i * 4, 4)].reshape(step, channels).astype(F32)
        v = v - jnp.mean(v, axis=-1, keepdims=True)
        v = v * lax.rsqrt(jnp.mean(v * v, axis=-1, keepdims=True) + 1e-05) * gain_ref[...].reshape(1, channels)
        at = pl.ds(pl.multiple_of(i * step, step), step)
        nb_ref[at, :] = v.astype(BF16)
        for k in range(channels // LANES):
            nf_ref[k, at, :] = v[:, cols(k)]
        return 0

    lax.fori_loop(0, tokens // step, norm, 0)
    for k in range(channels // LANES):
        strip_ref[0, :, cols(k)] = nf_ref[k, pl.ds(0, tr, stride=tc), :].astype(BF16)
        strip_ref[1, :, cols(k)] = nf_ref[k, pl.ds(tc - 1, tr, stride=tc), :].astype(BF16)
    top, bottom = nb_ref.at[pl.ds(0, tc)], nb_ref.at[pl.ds(tokens - tc, tc)]
    left, right = strip_ref.at[0], strip_ref.at[1]
    up, down = lax.rem(row + n - 1, n), lax.rem(row + 1, n)
    west, east = lax.rem(col + n - 1, n), lax.rem(col + 1, n)
    greeted()
    plan = (
        (bottom, down, col), (top, up, col), (right, row, east), (left, row, west),
        (bottom, down, east), (bottom, down, west), (top, up, east), (top, up, west),
    )
    halos = [
        remote(src, halo_ref.at[pl.ds(slot * tc, tc)], hs_sem.at[slot], hr_sem.at[slot], r, c)
        for slot, (src, r, c) in enumerate(plan)
    ]
    for copy in halos:
        copy.start()
    fetch[2].wait()

    def project(i, _):
        at = pl.ds(pl.multiple_of(i * step, step), step)
        inner = dot(nb_ref[at, :], wi_ref[:, :width]).astype(BF16).astype(F32)
        for k in range(groups):
            pad_ref[k, pl.ds(1 + i * 4, 4), 8 : 8 + tc, :] = inner[:, cols(k)].reshape(4, tc, LANES)
        return 0

    lax.fori_loop(0, tokens // step, project, 0)
    for copy in halos:
        copy.wait()
    edge = dot(halo_ref[...], wi_ref[:, :width]).astype(BF16).astype(F32)
    north, south = row > 0, row < n - 1
    lwest, least = col > 0, col < n - 1

    def seen(slot, ok, first=0, count=tc):
        return jnp.where(ok, edge[slot * tc + first : slot * tc + first + count], 0.0)

    n_all, s_all = seen(0, north), seen(1, south)
    w_all, e_all = seen(2, lwest), seen(3, least)
    nw, ne = seen(4, north & lwest, tc - 8, 8), seen(5, north & least, 0, 8)
    sw, se = seen(6, south & lwest, tc - 8, 8), seen(7, south & least, 0, 8)
    for k in range(groups):
        pad_ref[k, 0, 8 : 8 + tc, :] = n_all[:, cols(k)]
        pad_ref[k, tr + 1, 8 : 8 + tc, :] = s_all[:, cols(k)]
        pad_ref[k, 0, 0:8, :] = nw[:, cols(k)]
        pad_ref[k, 0, 8 + tc : 16 + tc, :] = ne[:, cols(k)]
        pad_ref[k, tr + 1, 0:8, :] = sw[:, cols(k)]
        pad_ref[k, tr + 1, 8 + tc : 16 + tc, :] = se[:, cols(k)]
        for r in range(tr):
            pad_ref[k, 1 + r, 7:8, :] = w_all[r : r + 1, cols(k)]
            pad_ref[k, 1 + r, 8 + tc : 9 + tc, :] = e_all[r : r + 1, cols(k)]
    fetch[3].wait()
    fetch[4].wait()
    bias = cb_ref[...].reshape(1, width)

    def row_tokens(r, to, which, owner):
        return remote(
            act_ref.at[r], line_ref.at[0, tile(which * half + owner)], ts_sem.at[0, r],
            tr_sem.at[0, which * half + owner], row, side * half + to,
        )

    def column_tokens(step, peer, owner):
        return remote(actt_ref.at[peer], line_ref.at[1, tile(owner)], ts_sem.at[1, step], tr_sem.at[1, owner], peer, col)

    def convolve(i, _):
        r = lax.rem(2 * seat + i, n)
        for k in range(groups):
            total = jnp.broadcast_to(bias[:, cols(k)], (tc, LANES))
            for a in range(3):
                for b in range(3):
                    total = total + pad_ref[k, r + a, 7 + b : 7 + b + tc, :] * cw_ref[a, b : b + 1, cols(k)]
            done = silu(total).astype(BF16)
            act_ref[r, :, cols(k)] = done
            actf_ref[k, tile(r), :] = done.astype(F32)

        @pl.when(i < n)
        def _():
            row_tokens(r, r // 2, lax.rem(r, 2), seat).start()

        return 0

    lax.fori_loop(2, n + 2, convolve, 0)

    def flip(j, _):
        for k in range(groups):
            actt_ref[j, :, cols(k)] = actf_ref[k, pl.ds(j, tr, stride=tc), :].astype(BF16)
        return 0

    lax.fori_loop(0, tc, flip, 0)
    others(lambda step, peer: column_tokens(step, peer, row).start())
    for which in range(2):
        line_ref[0, tile(which * half + seat), :] = act_ref[2 * seat + which]
    line_ref[1, tile(row), :] = actt_ref[row]

    def gates(i, _):
        at = pl.ds(pl.multiple_of(i * step, step), step)
        gate = dot(nb_ref[at, :], wi_ref[:, width:]).astype(BF16).astype(F32)
        gate_ref[at, :] = silu(gate)
        return 0

    lax.fori_loop(0, tokens // step, gates, 0)
    for i in range(5, len(fetch)):
        fetch[i].wait()

    def rates(d, _):
        for k in range(groups):
            dec_ref[d, k] = jnp.exp(dl_ref[d, :, cols(k)]) * -LOG2E
        return 0

    lax.fori_loop(0, dl_ref.shape[0], rates, 0)

    span = 16
    blocks = length // span
    held = (ha_ref, hb_ref)
    kk, cc = iota((3 * rank + states, span * states), 0), iota((3 * rank + states, span * states), 1)
    lane = iota((states, LANES), 1)

    def ready(line):
        def prepare(d, _):
            which = line * 2 + d
            repeat = (kk == 3 * rank + lax.rem(cc, states)).astype(BF16)
            slot = iota((length, span * states), 1) // states
            mask = lax.rem(iota((length, span * states), 0), span) == slot + d * (span - 1 - 2 * slot)
            u = line_ref[line]
            to_rank = pw_ref[which, :rank, :]
            p = dot_nt(u, jnp.concatenate([to_rank] * 3 + [pw_ref[which, rank + states :, :]], axis=0))
            high = p.astype(BF16)
            low = p - high.astype(F32)
            stacked = jnp.where(iota(p.shape, 1) < 2 * rank, high.astype(F32), low).astype(BF16)[:, : 3 * rank]
            mc_ref[d] = jnp.where(mask, dot(high, repeat), 0.0).astype(BF16)
            weight = sw_ref[which]
            swh = weight.astype(BF16)
            swl = (weight - swh.astype(F32)).astype(BF16)
            weights = jnp.concatenate([swh, swl, swh], axis=0)
            shift = sb_ref[pl.ds(which, 1), :]
            wide = PIECE * LANES
            for g in range(0, groups, PIECE):
                at = slice(g * LANES, g * LANES + wide)
                s = softplus(dot(stacked, weights[:, at]) + shift[:, at])
                du = s * line_ref[line, :, at].astype(F32)
                for k in range(PIECE):
                    s_ref[d, g + k] = s[:, cols(k)]
                    du_ref[d, g + k] = du[:, cols(k)]
            enter = dot_nt(pw_ref[which, rank : rank + states, :], u)
            ones = jnp.ones((LANES, LANES), BF16)
            for h in range(length // LANES):
                for g in range(0, LANES, span):
                    spread = [jnp.where(lane == g + i, enter[:, cols(h)], 0.0) for i in range(span)]
                    at = (h * LANES + g) * states
                    bb_ref[d, at : at + span * states, :] = dot(jnp.concatenate(spread, axis=0).astype(BF16), ones)
            return 0

        lax.fori_loop(0, 2, prepare, 0)
        skip = sk_ref[pl.ds(line * 2, 1), :] + sk_ref[pl.ds(line * 2 + 1, 1), :]

        def begin(i, _):
            at = pl.ds(pl.multiple_of(i * 32, 32), 32)
            v = line_ref[line, at, :].astype(F32) * skip
            for k in range(groups):
                acc_ref[k, at, :] = v[:, cols(k)]
            return 0

        lax.fori_loop(0, length // 32, begin, 0)

    def zeros(per):
        return tuple(tuple((jnp.zeros((8, LANES), F32),) * 2 for _ in range(per)) for _ in range(2))

    def run(per, g0, streams, blocks, init):
        dec = [
            [[dec_ref[w, g0 + k, 8 * v : 8 * v + 8, :] for v in range(2)] for k in range(per)] for w, _, _, _ in streams
        ]

        def low(i, q):
            _, _, first, back = streams[q]
            return pl.multiple_of(first + (i + back * (blocks - 1 - 2 * i)) * span, span)

        def leave(slot, i, q):
            b = low(i, q)
            states_now = jnp.concatenate([held[slot][q, k] for k in range(per)], axis=1)
            part = dot(mc_ref[streams[q][1], pl.ds(b, span), :], states_now)
            for k in range(per):
                acc_ref[g0 + k, pl.ds(b, span), :] += part[:, cols(k)]

        def advance(slot, i, h):
            for j in range(span):
                for q in range(2):
                    _, d, _, back = streams[q]
                    t = low(i, q) + (j + back * (span - 1 - 2 * j))
                    enter = [bb_ref[d, pl.ds(pl.multiple_of(t * states + 8 * v, 8), 8), :] for v in range(2)]
                    for k in range(per):
                        s = s_ref[d, g0 + k, pl.ds(t, 8, stride=0), :]
                        du = du_ref[d, g0 + k, pl.ds(t, 8, stride=0), :]
                        now = [jnp.exp2(s * dec[q][k][v]) * h[q][k][v] + du * enter[v] for v in range(2)]
                        h[q][k] = now
                        held[slot][q, k, j * states : (j + 1) * states, :] = jnp.concatenate(now, axis=0).astype(BF16)
            return h

        def body(i, h):
            h = [[list(v) for v in part] for part in h]
            for q in range(2):
                leave(1, jnp.maximum(2 * i - 1, 0), q)
            h = advance(0, 2 * i, h)
            for q in range(2):
                leave(0, 2 * i, q)
            h = advance(1, 2 * i + 1, h)
            return tuple(tuple(tuple(v) for v in part) for part in h)

        for q in range(2):
            for k in range(per):
                hb_ref[q, k] = jnp.zeros_like(hb_ref[q, k])
        h = lax.fori_loop(0, blocks // 2, body, init)
        for q in range(2):
            leave(1, blocks - 1, q)
        return h

    def settle(line, per, g0):
        for k in range(per):
            y_ref[line, g0 + k] = acc_ref[g0 + k].astype(BF16)

    def row_result(c, r, to, which, owner):
        at = pl.ds(c * PER[0], PER[0])
        return remote(
            y_ref.at[0, at, tile(which * half + to)], land_ref.at[0, at, 2 * owner + which], ys_sem.at[0, c, r],
            yr_sem.at[0, c, 2 * owner + which], row, side * half + to,
        )

    def column_result(c, step, peer, owner):
        at = pl.ds(c * PER[1], PER[1])
        return remote(
            y_ref.at[1, at, tile(peer)], land_ref.at[1, at, owner], ys_sem.at[1, c, step], yr_sem.at[1, c, owner],
            peer, col,
        )

    def state_copy(c):
        return remote(st_ref.at[c], sl_ref.at[c], ss_sem.at[c], sr_sem.at[c], row, lax.rem(col + half, n))

    def lines(d):
        return [(d, d, which * (length // 2), d) for which in range(2)]

    def outward(c, _):
        per = PER[0]
        h = run(per, c * per, lines(side), blocks // 2, zeros(per))
        for q in range(2):
            for k in range(per):
                st_ref[c, q, k] = jnp.concatenate(h[q][k], axis=0).astype(BF16)
        state_copy(c).start()
        return 0

    def inward(c, _):
        per = PER[0]
        state_copy(c).wait_recv()
        came = [[sl_ref[c, q, k].astype(F32) for k in range(per)] for q in range(2)]
        init = tuple(tuple((v[:8], v[8:]) for v in part) for part in came)
        run(per, c * per, lines(1 - side), blocks // 2, init)
        settle(0, per, c * per)
        mates(lambda r, to, which: row_result(c, r, to, which, seat).start())
        for k in range(per):
            for which in range(2):
                land_ref[0, c * per + k, 2 * seat + which] = y_ref[0, c * per + k, tile(which * half + seat), :]
        return 0

    def down_and_up(c, _):
        per = PER[1]
        run(per, c * per, [(2, 0, 0, 0), (3, 1, 0, 1)], blocks, zeros(per))
        settle(1, per, c * per)
        others(lambda step, peer: column_result(c, step, peer, row).start())
        for k in range(per):
            land_ref[1, c * per + k, row] = y_ref[1, c * per + k, tile(row), :]
        return 0

    mates(lambda r, to, which: row_tokens(r, to, which, to).wait_recv())
    ready(0)
    lax.fori_loop(0, groups // PER[0], outward, 0)
    lax.fori_loop(0, groups // PER[0], inward, 0)
    others(lambda step, peer: column_tokens(step, peer, peer).wait_recv())
    ready(1)
    lax.fori_loop(0, groups // PER[1], down_and_up, 0)
    mates(lambda r, to, which: row_tokens(r, to, which, seat).wait_send())
    others(lambda step, peer: column_tokens(step, peer, row).wait_send())
    for c in range(groups // PER[0]):
        state_copy(c).wait_send()
        mates(lambda r, to, which: row_result(c, r, to, which, to).wait_recv())
    for c in range(groups // PER[1]):
        others(lambda step, peer: column_result(c, step, peer, peer).wait_recv())

        def widen(j, _):
            for k in range(c * PER[1], (c + 1) * PER[1]):
                cf_ref[k, tile(j), :] = land_ref[1, k, j].astype(F32)
            return 0

        lax.fori_loop(0, tc, widen, 0)

    def finish(r, _):
        other = jnp.concatenate([cf_ref[k, pl.ds(r, tc, stride=tr), :] for k in range(groups)], axis=1)
        v = jnp.concatenate([land_ref[0, k, r] for k in range(groups)], axis=1).astype(F32) + other
        v = v - jnp.mean(v, axis=-1, keepdims=True)
        v = v * lax.rsqrt(jnp.mean(v * v, axis=-1, keepdims=True) + 1e-05) * og_ref[...].reshape(1, width)
        go_ref[tile(r), :] = (v * gate_ref[tile(r), :]).astype(BF16)
        return 0

    lax.fori_loop(0, tr, finish, 0)
    out_ref[...] = dot(go_ref[...], wo_ref[...]).astype(BF16).reshape(out_ref.shape)

    for c in range(groups // PER[0]):
        mates(lambda r, to, which: row_result(c, r, to, which, seat).wait_send())
    for c in range(groups // PER[1]):
        others(lambda step, peer: column_result(c, step, peer, row).wait_send())


def local(
    n, features, norm_gain, in_weight, conv_weight, conv_bias, proj_weight, step_weight, step_bias,
    decay_log, skip_gain, out_gain, out_weight,
):
    tr, tc, channels = features.shape
    width = out_weight.shape[0]
    tokens = tr * tc
    groups = width // LANES
    length = tc * n
    dma = pltpu.SemaphoreType.DMA
    pw = jnp.swapaxes(proj_weight, 1, 2)
    dl = jnp.swapaxes(decay_log, 1, 2)
    states = dl.shape[1]
    span, per = 16, max(PER)
    chunks = groups // min(PER)
    hbm = pl.BlockSpec(memory_space=pltpu.HBM)
    operands = (
        features, norm_gain, in_weight, conv_weight, conv_bias, pw, step_weight, step_bias, dl, skip_gain,
        out_gain, out_weight,
    )
    return pl.pallas_call(
        functools.partial(block_kernel, n),
        out_shape=jax.ShapeDtypeStruct(features.shape, BF16),
        in_specs=[hbm] * len(operands),
        out_specs=VMEM,
        scratch_shapes=[pltpu.VMEM(a.shape, a.dtype) for a in operands] + [
            pltpu.VMEM((tokens, channels), BF16),
            pltpu.VMEM((channels // LANES, tokens, LANES), F32),
            pltpu.VMEM((2, tr, channels), BF16),
            pltpu.VMEM((8 * tc, channels), BF16),
            pltpu.VMEM((groups, tr + 2, tc + 16, LANES), F32),
            pltpu.VMEM((tr, tc, width), BF16),
            pltpu.VMEM((tc, tr, width), BF16),
            pltpu.VMEM((groups, tokens, LANES), F32),
            pltpu.VMEM((2, length, width), BF16),
            pltpu.VMEM((tokens, width), F32),
            pltpu.VMEM((2, groups, length, LANES), F32),
            pltpu.VMEM((2, groups, length, LANES), F32),
            pltpu.VMEM((2, length * states, LANES), F32),
            pltpu.VMEM((2, length, span * states), BF16),
            pltpu.VMEM((dl.shape[0], groups, states, LANES), F32),
            pltpu.VMEM((2, per, span * states, LANES), BF16),
            pltpu.VMEM((2, per, span * states, LANES), BF16),
            pltpu.VMEM((groups, length, LANES), F32),
            pltpu.VMEM((2, groups, length, LANES), BF16),
            pltpu.VMEM((2, groups, n, tc, LANES), BF16),
            pltpu.VMEM((groups, tokens, LANES), F32),
            pltpu.VMEM((tokens, width), BF16),
            pltpu.VMEM((groups // PER[0], 2, PER[0], states, LANES), BF16),
            pltpu.VMEM((groups // PER[0], 2, PER[0], states, LANES), BF16),
            dma((len(operands),)), dma((8,)), dma((8,)), dma((2, n)), dma((2, n)), dma((2, chunks, n)), dma((2, chunks, n)),
            dma((groups // PER[0],)), dma((groups // PER[0],)),
        ],
        compiler_params=pltpu.CompilerParams(collective_id=0, has_side_effects=True, vmem_limit_bytes=60 << 20),
    )(*operands)


def solution(mesh):
    n = mesh.shape["row"]
    assert mesh.shape["col"] == n
    in_specs = (P("row", "col", None), P(), P(), P(), P(), P(), P(), P(), P(), P(), P(), P())
    return jax.shard_map(
        functools.partial(local, n), mesh=mesh, in_specs=in_specs, out_specs=P("row", "col", None), check_vma=False
    )
```

```python
import functools

import jax
import jax.numpy as jnp
from jax import lax
from jax.experimental import pallas as pl
from jax.experimental.pallas import tpu as pltpu
from jax.sharding import PartitionSpec as P

F32 = jnp.float32
BF16 = jnp.bfloat16
MESH = pl.DeviceIdType.MESH
NT = (((1,), (1,)), ((), ()))
LANES = 128
LOG2E = 1.4426950408889634
PIECE = 2
PER = (3, 3)
VMEM = pl.BlockSpec(memory_space=pltpu.VMEM)


def dot(a, b):
    return jnp.dot(a, b, preferred_element_type=F32)


def dot_nt(a, b):
    return lax.dot_general(a, b, NT, preferred_element_type=F32)


def softplus(z):
    w = jnp.exp2(jnp.abs(z) * -LOG2E)
    small = w * (1.0 - w * (0.5 - w * (1.0 / 3.0)))
    return jnp.maximum(z, 0.0) + jnp.where(w < 0.01, small, jnp.log(1.0 + w))


def silu(v):
    return v / (1.0 + jnp.exp(-v))


def iota(shape, dim):
    return lax.broadcasted_iota(jnp.int32, shape, dim)


def cols(k):
    return slice(k * LANES, (k + 1) * LANES)


def place():
    return lax.axis_index("row"), lax.axis_index("col")


def greet(nr, nc):
    row, col = place()
    sem = pltpu.get_barrier_semaphore()

    def signal(r, c):
        pl.semaphore_signal(sem, inc=1, device_id={"row": r, "col": c}, device_id_type=MESH)

    def along_col(k, _):
        signal(row, lax.rem(col + k, nc))
        return 0

    def along_row(k, _):
        signal(lax.rem(row + k, nr), col)
        return 0

    lax.fori_loop(1, nc, along_col, 0)
    lax.fori_loop(1, nr, along_row, 0)
    for dr in (1, nr - 1):
        for dc in (1, nc - 1):
            signal(lax.rem(row + dr, nr), lax.rem(col + dc, nc))
    return lambda: pl.semaphore_wait(sem, nr + nc + 2)


def remote(src, dst, send_sem, recv_sem, r, c):
    return pltpu.make_async_remote_copy(
        src_ref=src, dst_ref=dst, send_sem=send_sem, recv_sem=recv_sem,
        device_id={"row": r, "col": c}, device_id_type=MESH,
    )


def block_kernel(
    n, x_hbm, gain_hbm, wi_hbm, cw_hbm, cb_hbm, pw_hbm, sw_hbm, sb_hbm, dl_hbm, sk_hbm, og_hbm, wo_hbm, out_ref,
    x_ref, gain_ref, wi_ref, cw_ref, cb_ref, pw_ref, sw_ref, sb_ref, dl_ref, sk_ref, og_ref, wo_ref,
    nb_ref, nf_ref, strip_ref, halo_ref, pad_ref, act_ref, actt_ref, actf_ref, line_ref, gate_ref,
    s_ref, du_ref, bb_ref, mc_ref, dec_ref, ha_ref, hb_ref, acc_ref, y_ref, land_ref, cf_ref, go_ref,
    st_ref, sl_ref, own_sem, hs_sem, hr_sem, ts_sem, tr_sem, ys_sem, yr_sem, ss_sem, sr_sem,
):
    tr, tc, channels = x_ref.shape
    width = cb_ref.shape[-1]
    tokens = tr * tc
    groups = width // LANES
    length = line_ref.shape[1]
    rank, states = sw_ref.shape[1], dl_ref.shape[1]
    row, col = place()
    there = (x_hbm, gain_hbm, wi_hbm, cw_hbm, cb_hbm, pw_hbm, sw_hbm, sb_hbm, dl_hbm, sk_hbm, og_hbm, wo_hbm)
    here = (x_ref, gain_ref, wi_ref, cw_ref, cb_ref, pw_ref, sw_ref, sb_ref, dl_ref, sk_ref, og_ref, wo_ref)
    fetch = [pltpu.make_async_copy(src, dst, own_sem.at[i]) for i, (src, dst) in enumerate(zip(there, here))]
    for copy in fetch:
        copy.start()
    greeted = greet(n, n)

    half = n // 2
    side, seat = col // half, lax.rem(col, half)

    def others(one):
        def body(step, _):
            one(step, lax.rem(row + step, n))
            return 0

        lax.fori_loop(1, n, body, 0)

    def mates(one):
        def body(step, _):
            r = lax.rem(2 * seat + step, n)
            one(r, r // 2, lax.rem(r, 2))
            return 0

        lax.fori_loop(2, n, body, 0)

    def tile(i):
        return pl.ds(pl.multiple_of(i * tc, tc), tc)

    step = 4 * tc
    fetch[0].wait()
    fetch[1].wait()

    def norm(i, _):
        v = x_ref[pl.ds(i * 4, 4)].reshape(step, channels).astype(F32)
        v = v - jnp.mean(v, axis=-1, keepdims=True)
        v = v * lax.rsqrt(jnp.mean(v * v, axis=-1, keepdims=True) + 1e-05) * gain_ref[...].reshape(1, channels)
        at = pl.ds(pl.multiple_of(i * step, step), step)
        nb_ref[at, :] = v.astype(BF16)
        for k in range(channels // LANES):
            nf_ref[k, at, :] = v[:, cols(k)]
        return 0

    lax.fori_loop(0, tokens // step, norm, 0)
    for k in range(channels // LANES):
        strip_ref[0, :, cols(k)] = nf_ref[k, pl.ds(0, tr, stride=tc), :].astype(BF16)
        strip_ref[1, :, cols(k)] = nf_ref[k, pl.ds(tc - 1, tr, stride=tc), :].astype(BF16)
    top, bottom = nb_ref.at[pl.ds(0, tc)], nb_ref.at[pl.ds(tokens - tc, tc)]
    left, right = strip_ref.at[0], strip_ref.at[1]
    up, down = lax.rem(row + n - 1, n), lax.rem(row + 1, n)
    west, east = lax.rem(col + n - 1, n), lax.rem(col + 1, n)
    greeted()
    plan = (
        (bottom, down, col), (top, up, col), (right, row, east), (left, row, west),
        (bottom, down, east), (bottom, down, west), (top, up, east), (top, up, west),
    )
    halos = [
        remote(src, halo_ref.at[pl.ds(slot * tc, tc)], hs_sem.at[slot], hr_sem.at[slot], r, c)
        for slot, (src, r, c) in enumerate(plan)
    ]
    for copy in halos:
        copy.start()
    fetch[2].wait()

    def project(i, _):
        at = pl.ds(pl.multiple_of(i * step, step), step)
        inner = dot(nb_ref[at, :], wi_ref[:, :width]).astype(BF16).astype(F32)
        for k in range(groups):
            pad_ref[k, pl.ds(1 + i * 4, 4), 8 : 8 + tc, :] = inner[:, cols(k)].reshape(4, tc, LANES)
        return 0

    lax.fori_loop(0, tokens // step, project, 0)
    for copy in halos:
        copy.wait()
    edge = dot(halo_ref[...], wi_ref[:, :width]).astype(BF16).astype(F32)
    north, south = row > 0, row < n - 1
    lwest, least = col > 0, col < n - 1

    def seen(slot, ok, first=0, count=tc):
        return jnp.where(ok, edge[slot * tc + first : slot * tc + first + count], 0.0)

    n_all, s_all = seen(0, north), seen(1, south)
    w_all, e_all = seen(2, lwest), seen(3, least)
    nw, ne = seen(4, north & lwest, tc - 8, 8), seen(5, north & least, 0, 8)
    sw, se = seen(6, south & lwest, tc - 8, 8), seen(7, south & least, 0, 8)
    for k in range(groups):
        pad_ref[k, 0, 8 : 8 + tc, :] = n_all[:, cols(k)]
        pad_ref[k, tr + 1, 8 : 8 + tc, :] = s_all[:, cols(k)]
        pad_ref[k, 0, 0:8, :] = nw[:, cols(k)]
        pad_ref[k, 0, 8 + tc : 16 + tc, :] = ne[:, cols(k)]
        pad_ref[k, tr + 1, 0:8, :] = sw[:, cols(k)]
        pad_ref[k, tr + 1, 8 + tc : 16 + tc, :] = se[:, cols(k)]
        for r in range(tr):
            pad_ref[k, 1 + r, 7:8, :] = w_all[r : r + 1, cols(k)]
            pad_ref[k, 1 + r, 8 + tc : 9 + tc, :] = e_all[r : r + 1, cols(k)]
    fetch[3].wait()
    fetch[4].wait()
    bias = cb_ref[...].reshape(1, width)

    def row_tokens(r, to, which, owner):
        return remote(
            act_ref.at[r], line_ref.at[0, tile(which * half + owner)], ts_sem.at[0, r],
            tr_sem.at[0, which * half + owner], row, side * half + to,
        )

    def column_tokens(step, peer, owner):
        return remote(actt_ref.at[peer], line_ref.at[1, tile(owner)], ts_sem.at[1, step], tr_sem.at[1, owner], peer, col)

    def convolve(i, _):
        r = lax.rem(2 * seat + i, n)
        for k in range(groups):
            total = jnp.broadcast_to(bias[:, cols(k)], (tc, LANES))
            for a in range(3):
                for b in range(3):
                    total = total + pad_ref[k, r + a, 7 + b : 7 + b + tc, :] * cw_ref[a, b : b + 1, cols(k)]
            done = silu(total).astype(BF16)
            act_ref[r, :, cols(k)] = done
            actf_ref[k, tile(r), :] = done.astype(F32)

        @pl.when(i < n)
        def _():
            row_tokens(r, r // 2, lax.rem(r, 2), seat).start()

        return 0

    lax.fori_loop(2, n + 2, convolve, 0)

    def flip(j, _):
        for k in range(groups):
            actt_ref[j, :, cols(k)] = actf_ref[k, pl.ds(j, tr, stride=tc), :].astype(BF16)
        return 0

    lax.fori_loop(0, tc, flip, 0)
    others(lambda step, peer: column_tokens(step, peer, row).start())
    for which in range(2):
        line_ref[0, tile(which * half + seat), :] = act_ref[2 * seat + which]
    line_ref[1, tile(row), :] = actt_ref[row]

    def gates(i, _):
        at = pl.ds(pl.multiple_of(i * step, step), step)
        gate = dot(nb_ref[at, :], wi_ref[:, width:]).astype(BF16).astype(F32)
        gate_ref[at, :] = silu(gate)
        return 0

    lax.fori_loop(0, tokens // step, gates, 0)
    for i in range(5, len(fetch)):
        fetch[i].wait()

    def rates(d, _):
        for k in range(groups):
            dec_ref[d, k] = jnp.exp(dl_ref[d, :, cols(k)]) * -LOG2E
        return 0

    lax.fori_loop(0, dl_ref.shape[0], rates, 0)

    span = 16
    blocks = length // span
    held = (ha_ref, hb_ref)
    kk, cc = iota((3 * rank + states, span * states), 0), iota((3 * rank + states, span * states), 1)
    lane = iota((states, LANES), 1)

    def ready(line):
        def prepare(d, _):
            which = line * 2 + d
            repeat = (kk == 3 * rank + lax.rem(cc, states)).astype(BF16)
            slot = iota((length, span * states), 1) // states
            mask = lax.rem(iota((length, span * states), 0), span) == slot + d * (span - 1 - 2 * slot)
            u = line_ref[line]
            to_rank = pw_ref[which, :rank, :]
            p = dot_nt(u, jnp.concatenate([to_rank] * 3 + [pw_ref[which, rank + states :, :]], axis=0))
            high = p.astype(BF16)
            low = p - high.astype(F32)
            stacked = jnp.where(iota(p.shape, 1) < 2 * rank, high.astype(F32), low).astype(BF16)[:, : 3 * rank]
            mc_ref[line, d] = jnp.where(mask, dot(high, repeat), 0.0).astype(BF16)
            weight = sw_ref[which]
            swh = weight.astype(BF16)
            swl = (weight - swh.astype(F32)).astype(BF16)
            weights = jnp.concatenate([swh, swl, swh], axis=0)
            shift = sb_ref[pl.ds(which, 1), :]
            wide = PIECE * LANES
            for g in range(0, groups, PIECE):
                at = slice(g * LANES, g * LANES + wide)
                s = softplus(dot(stacked, weights[:, at]) + shift[:, at])
                du = s * line_ref[line, :, at].astype(F32)
                for k in range(PIECE):
                    s_ref[line, d, g + k] = s[:, cols(k)]
                    du_ref[line, d, g + k] = du[:, cols(k)]
            enter = dot_nt(pw_ref[which, rank : rank + states, :], u)
            ones = jnp.ones((LANES, LANES), BF16)
            for h in range(length // LANES):
                for g in range(0, LANES, span):
                    spread = [jnp.where(lane == g + i, enter[:, cols(h)], 0.0) for i in range(span)]
                    at = (h * LANES + g) * states
                    bb_ref[line, d, at : at + span * states, :] = dot(jnp.concatenate(spread, axis=0).astype(BF16), ones)
            return 0

        lax.fori_loop(0, 2, prepare, 0)
        skip = sk_ref[pl.ds(line * 2, 1), :] + sk_ref[pl.ds(line * 2 + 1, 1), :]

        def begin(i, _):
            at = pl.ds(pl.multiple_of(i * 32, 32), 32)
            v = line_ref[line, at, :].astype(F32) * skip
            for k in range(groups):
                acc_ref[line, k, at, :] = v[:, cols(k)]
            return 0

        lax.fori_loop(0, length // 32, begin, 0)

    def zeros(per):
        return tuple(tuple((jnp.zeros((8, LANES), F32),) * 2 for _ in range(per)) for _ in range(2))

    def run(line, per, g0, streams, blocks, init):
        dec = [
            [[dec_ref[w, g0 + k, 8 * v : 8 * v + 8, :] for v in range(2)] for k in range(per)] for w, _, _, _ in streams
        ]

        def low(i, q):
            _, _, first, back = streams[q]
            return pl.multiple_of(first + (i + back * (blocks - 1 - 2 * i)) * span, span)

        def leave(slot, i, q):
            b = low(i, q)
            states_now = jnp.concatenate([held[slot][q, k] for k in range(per)], axis=1)
            part = dot(mc_ref[line, streams[q][1], pl.ds(b, span), :], states_now)
            for k in range(per):
                acc_ref[line, g0 + k, pl.ds(b, span), :] += part[:, cols(k)]

        def advance(slot, i, h):
            for j in range(span):
                for q in range(2):
                    _, d, _, back = streams[q]
                    t = low(i, q) + (j + back * (span - 1 - 2 * j))
                    enter = [bb_ref[line, d, pl.ds(pl.multiple_of(t * states + 8 * v, 8), 8), :] for v in range(2)]
                    for k in range(per):
                        s = s_ref[line, d, g0 + k, pl.ds(t, 8, stride=0), :]
                        du = du_ref[line, d, g0 + k, pl.ds(t, 8, stride=0), :]
                        now = [jnp.exp2(s * dec[q][k][v]) * h[q][k][v] + du * enter[v] for v in range(2)]
                        h[q][k] = now
                        held[slot][q, k, j * states : (j + 1) * states, :] = jnp.concatenate(now, axis=0).astype(BF16)
            return h

        def body(i, h):
            h = [[list(v) for v in part] for part in h]
            for q in range(2):
                leave(1, jnp.maximum(2 * i - 1, 0), q)
            h = advance(0, 2 * i, h)
            for q in range(2):
                leave(0, 2 * i, q)
            h = advance(1, 2 * i + 1, h)
            return tuple(tuple(tuple(v) for v in part) for part in h)

        for q in range(2):
            for k in range(per):
                hb_ref[q, k] = jnp.zeros_like(hb_ref[q, k])
        h = lax.fori_loop(0, blocks // 2, body, init)
        for q in range(2):
            leave(1, blocks - 1, q)
        return h

    def settle(line, per, g0):
        for k in range(per):
            y_ref[line, g0 + k] = acc_ref[line, g0 + k].astype(BF16)

    def row_result(c, r, to, which, owner):
        at = pl.ds(c * PER[0], PER[0])
        return remote(
            y_ref.at[0, at, tile(which * half + to)], land_ref.at[0, at, 2 * owner + which], ys_sem.at[0, c, r],
            yr_sem.at[0, c, 2 * owner + which], row, side * half + to,
        )

    def column_result(c, step, peer, owner):
        at = pl.ds(c * PER[1], PER[1])
        return remote(
            y_ref.at[1, at, tile(peer)], land_ref.at[1, at, owner], ys_sem.at[1, c, step], yr_sem.at[1, c, owner],
            peer, col,
        )

    def state_copy(c):
        return remote(st_ref.at[c], sl_ref.at[c], ss_sem.at[c], sr_sem.at[c], row, lax.rem(col + half, n))

    def lines(d):
        return [(d, d, which * (length // 2), d) for which in range(2)]

    def outward(c, _):
        per = PER[0]
        h = run(0, per, c * per, lines(side), blocks // 2, zeros(per))
        for q in range(2):
            for k in range(per):
                st_ref[c, q, k] = jnp.concatenate(h[q][k], axis=0).astype(BF16)
        state_copy(c).start()
        return 0

    def inward(c, _):
        per = PER[0]
        state_copy(c).wait_recv()
        came = [[sl_ref[c, q, k].astype(F32) for k in range(per)] for q in range(2)]
        init = tuple(tuple((v[:8], v[8:]) for v in part) for part in came)
        run(0, per, c * per, lines(1 - side), blocks // 2, init)
        settle(0, per, c * per)
        mates(lambda r, to, which: row_result(c, r, to, which, seat).start())
        for k in range(per):
            for which in range(2):
                land_ref[0, c * per + k, 2 * seat + which] = y_ref[0, c * per + k, tile(which * half + seat), :]
        return 0

    def down_and_up(c, _):
        per = PER[1]
        run(1, per, c * per, [(2, 0, 0, 0), (3, 1, 0, 1)], blocks, zeros(per))
        settle(1, per, c * per)
        others(lambda step, peer: column_result(c, step, peer, row).start())
        for k in range(per):
            land_ref[1, c * per + k, row] = y_ref[1, c * per + k, tile(row), :]
        return 0

    mates(lambda r, to, which: row_tokens(r, to, which, to).wait_recv())
    ready(0)
    lax.fori_loop(0, groups // PER[0], outward, 0)
    others(lambda step, peer: column_tokens(step, peer, peer).wait_recv())
    ready(1)
    lax.fori_loop(0, groups // PER[1], down_and_up, 0)
    lax.fori_loop(0, groups // PER[0], inward, 0)
    mates(lambda r, to, which: row_tokens(r, to, which, seat).wait_send())
    others(lambda step, peer: column_tokens(step, peer, row).wait_send())
    for c in range(groups // PER[0]):
        state_copy(c).wait_send()
        mates(lambda r, to, which: row_result(c, r, to, which, to).wait_recv())
    for c in range(groups // PER[1]):
        others(lambda step, peer: column_result(c, step, peer, peer).wait_recv())

        def widen(j, _):
            for k in range(c * PER[1], (c + 1) * PER[1]):
                cf_ref[k, tile(j), :] = land_ref[1, k, j].astype(F32)
            return 0

        lax.fori_loop(0, tc, widen, 0)

    def finish(r, _):
        other = jnp.concatenate([cf_ref[k, pl.ds(r, tc, stride=tr), :] for k in range(groups)], axis=1)
        v = jnp.concatenate([land_ref[0, k, r] for k in range(groups)], axis=1).astype(F32) + other
        v = v - jnp.mean(v, axis=-1, keepdims=True)
        v = v * lax.rsqrt(jnp.mean(v * v, axis=-1, keepdims=True) + 1e-05) * og_ref[...].reshape(1, width)
        go_ref[tile(r), :] = (v * gate_ref[tile(r), :]).astype(BF16)
        return 0

    lax.fori_loop(0, tr, finish, 0)
    out_ref[...] = dot(go_ref[...], wo_ref[...]).astype(BF16).reshape(out_ref.shape)

    for c in range(groups // PER[0]):
        mates(lambda r, to, which: row_result(c, r, to, which, seat).wait_send())
    for c in range(groups // PER[1]):
        others(lambda step, peer: column_result(c, step, peer, row).wait_send())


def local(
    n, features, norm_gain, in_weight, conv_weight, conv_bias, proj_weight, step_weight, step_bias,
    decay_log, skip_gain, out_gain, out_weight,
):
    tr, tc, channels = features.shape
    width = out_weight.shape[0]
    tokens = tr * tc
    groups = width // LANES
    length = tc * n
    dma = pltpu.SemaphoreType.DMA
    pw = jnp.swapaxes(proj_weight, 1, 2)
    dl = jnp.swapaxes(decay_log, 1, 2)
    states = dl.shape[1]
    span, per = 16, max(PER)
    chunks = groups // min(PER)
    hbm = pl.BlockSpec(memory_space=pltpu.HBM)
    operands = (
        features, norm_gain, in_weight, conv_weight, conv_bias, pw, step_weight, step_bias, dl, skip_gain,
        out_gain, out_weight,
    )
    return pl.pallas_call(
        functools.partial(block_kernel, n),
        out_shape=jax.ShapeDtypeStruct(features.shape, BF16),
        in_specs=[hbm] * len(operands),
        out_specs=VMEM,
        scratch_shapes=[pltpu.VMEM(a.shape, a.dtype) for a in operands] + [
            pltpu.VMEM((tokens, channels), BF16),
            pltpu.VMEM((channels // LANES, tokens, LANES), F32),
            pltpu.VMEM((2, tr, channels), BF16),
            pltpu.VMEM((8 * tc, channels), BF16),
            pltpu.VMEM((groups, tr + 2, tc + 16, LANES), F32),
            pltpu.VMEM((tr, tc, width), BF16),
            pltpu.VMEM((tc, tr, width), BF16),
            pltpu.VMEM((groups, tokens, LANES), F32),
            pltpu.VMEM((2, length, width), BF16),
            pltpu.VMEM((tokens, width), F32),
            pltpu.VMEM((2, 2, groups, length, LANES), F32),
            pltpu.VMEM((2, 2, groups, length, LANES), F32),
            pltpu.VMEM((2, 2, length * states, LANES), F32),
            pltpu.VMEM((2, 2, length, span * states), BF16),
            pltpu.VMEM((dl.shape[0], groups, states, LANES), F32),
            pltpu.VMEM((2, per, span * states, LANES), BF16),
            pltpu.VMEM((2, per, span * states, LANES), BF16),
            pltpu.VMEM((2, groups, length, LANES), F32),
            pltpu.VMEM((2, groups, length, LANES), BF16),
            pltpu.VMEM((2, groups, n, tc, LANES), BF16),
            pltpu.VMEM((groups, tokens, LANES), F32),
            pltpu.VMEM((tokens, width), BF16),
            pltpu.VMEM((groups // PER[0], 2, PER[0], states, LANES), BF16),
            pltpu.VMEM((groups // PER[0], 2, PER[0], states, LANES), BF16),
            dma((len(operands),)), dma((8,)), dma((8,)), dma((2, n)), dma((2, n)), dma((2, chunks, n)), dma((2, chunks, n)),
            dma((groups // PER[0],)), dma((groups // PER[0],)),
        ],
        compiler_params=pltpu.CompilerParams(collective_id=0, has_side_effects=True, vmem_limit_bytes=60 << 20),
    )(*operands)


def solution(mesh):
    n = mesh.shape["row"]
    assert mesh.shape["col"] == n
    in_specs = (P("row", "col", None), P(), P(), P(), P(), P(), P(), P(), P(), P(), P(), P())
    return jax.shard_map(
        functools.partial(local, n), mesh=mesh, in_specs=in_specs, out_specs=P("row", "col", None), check_vma=False
    )
```

```python
import functools

import jax
import jax.numpy as jnp
from jax import lax
from jax.experimental import pallas as pl
from jax.experimental.pallas import tpu as pltpu
from jax.sharding import PartitionSpec as P

F32 = jnp.float32
BF16 = jnp.bfloat16
MESH = pl.DeviceIdType.MESH
NT = (((1,), (1,)), ((), ()))
LANES = 128
LOG2E = 1.4426950408889634
PIECE = 2
PER = (3, 3)
VMEM = pl.BlockSpec(memory_space=pltpu.VMEM)


def dot(a, b):
    return jnp.dot(a, b, preferred_element_type=F32)


def dot_nt(a, b):
    return lax.dot_general(a, b, NT, preferred_element_type=F32)


def softplus(z):
    w = jnp.exp2(jnp.abs(z) * -LOG2E)
    small = w * (1.0 - w * (0.5 - w * (1.0 / 3.0)))
    return jnp.maximum(z, 0.0) + jnp.where(w < 0.01, small, jnp.log(1.0 + w))


def silu(v):
    return v / (1.0 + jnp.exp(-v))


def iota(shape, dim):
    return lax.broadcasted_iota(jnp.int32, shape, dim)


def cols(k):
    return slice(k * LANES, (k + 1) * LANES)


def place():
    return lax.axis_index("row"), lax.axis_index("col")


def greet(nr, nc):
    row, col = place()
    sem = pltpu.get_barrier_semaphore()

    def signal(r, c):
        pl.semaphore_signal(sem, inc=1, device_id={"row": r, "col": c}, device_id_type=MESH)

    def along_col(k, _):
        signal(row, lax.rem(col + k, nc))
        return 0

    def along_row(k, _):
        signal(lax.rem(row + k, nr), col)
        return 0

    lax.fori_loop(1, nc, along_col, 0)
    lax.fori_loop(1, nr, along_row, 0)
    for dr in (1, nr - 1):
        for dc in (1, nc - 1):
            signal(lax.rem(row + dr, nr), lax.rem(col + dc, nc))
    return lambda: pl.semaphore_wait(sem, nr + nc + 2)


def remote(src, dst, send_sem, recv_sem, r, c):
    return pltpu.make_async_remote_copy(
        src_ref=src, dst_ref=dst, send_sem=send_sem, recv_sem=recv_sem,
        device_id={"row": r, "col": c}, device_id_type=MESH,
    )


def block_kernel(
    n, x_hbm, gain_hbm, wi_hbm, cw_hbm, cb_hbm, pw_hbm, sw_hbm, sb_hbm, dl_hbm, sk_hbm, og_hbm, wo_hbm, out_ref,
    x_ref, gain_ref, wi_ref, cw_ref, cb_ref, pw_ref, sw_ref, sb_ref, dl_ref, sk_ref, og_ref, wo_ref,
    nb_ref, nf_ref, strip_ref, halo_ref, pad_ref, act_ref, actt_ref, actf_ref, line_ref, gate_ref,
    s_ref, du_ref, bb_ref, mc_ref, dec_ref, ha_ref, hb_ref, acc_ref, y_ref, land_ref, cf_ref, go_ref,
    st_ref, sl_ref, own_sem, hs_sem, hr_sem, ts_sem, tr_sem, ys_sem, yr_sem, ss_sem, sr_sem,
):
    tr, tc, channels = x_ref.shape
    width = cb_ref.shape[-1]
    tokens = tr * tc
    groups = width // LANES
    length = line_ref.shape[1]
    rank, states = sw_ref.shape[1], dl_ref.shape[1]
    row, col = place()
    there = (x_hbm, gain_hbm, wi_hbm, cw_hbm, cb_hbm, pw_hbm, sw_hbm, sb_hbm, dl_hbm, sk_hbm, og_hbm, wo_hbm)
    here = (x_ref, gain_ref, wi_ref, cw_ref, cb_ref, pw_ref, sw_ref, sb_ref, dl_ref, sk_ref, og_ref, wo_ref)
    fetch = [pltpu.make_async_copy(src, dst, own_sem.at[i]) for i, (src, dst) in enumerate(zip(there, here))]
    fetch[0].start()
    greeted = greet(n, n)
    for copy in fetch[1:]:
        copy.start()

    half = n // 2
    side, seat = col // half, lax.rem(col, half)

    def others(one):
        def body(step, _):
            one(step, lax.rem(row + step, n))
            return 0

        lax.fori_loop(1, n, body, 0)

    def mates(one):
        def body(step, _):
            r = lax.rem(2 * seat + step, n)
            one(r, r // 2, lax.rem(r, 2))
            return 0

        lax.fori_loop(2, n, body, 0)

    def tile(i):
        return pl.ds(pl.multiple_of(i * tc, tc), tc)

    step = 4 * tc
    fetch[0].wait()
    fetch[1].wait()

    def norm(i, _):
        v = x_ref[pl.ds(i * 4, 4)].reshape(step, channels).astype(F32)
        v = v - jnp.mean(v, axis=-1, keepdims=True)
        v = v * lax.rsqrt(jnp.mean(v * v, axis=-1, keepdims=True) + 1e-05) * gain_ref[...].reshape(1, channels)
        at = pl.ds(pl.multiple_of(i * step, step), step)
        nb_ref[at, :] = v.astype(BF16)
        for k in range(channels // LANES):
            nf_ref[k, at, :] = v[:, cols(k)]
        return 0

    hb_ref[...] = jnp.zeros_like(hb_ref)
    lax.fori_loop(0, tokens // step, norm, 0, unroll=2)
    for k in range(channels // LANES):
        strip_ref[0, :, cols(k)] = nf_ref[k, pl.ds(0, tr, stride=tc), :].astype(BF16)
        strip_ref[1, :, cols(k)] = nf_ref[k, pl.ds(tc - 1, tr, stride=tc), :].astype(BF16)
    top, bottom = nb_ref.at[pl.ds(0, tc)], nb_ref.at[pl.ds(tokens - tc, tc)]
    left, right = strip_ref.at[0], strip_ref.at[1]
    up, down = lax.rem(row + n - 1, n), lax.rem(row + 1, n)
    west, east = lax.rem(col + n - 1, n), lax.rem(col + 1, n)
    greeted()
    plan = (
        (bottom, down, col), (top, up, col), (right, row, east), (left, row, west),
        (bottom, down, east), (bottom, down, west), (top, up, east), (top, up, west),
    )
    halos = [
        remote(src, halo_ref.at[pl.ds(slot * tc, tc)], hs_sem.at[slot], hr_sem.at[slot], r, c)
        for slot, (src, r, c) in enumerate(plan)
    ]
    for copy in halos:
        copy.start()
    fetch[2].wait()

    def project(i, _):
        at = pl.ds(pl.multiple_of(i * step, step), step)
        inner = dot(nb_ref[at, :], wi_ref[:, :width]).astype(BF16).astype(F32)
        for k in range(groups):
            pad_ref[k, pl.ds(1 + i * 4, 4), 8 : 8 + tc, :] = inner[:, cols(k)].reshape(4, tc, LANES)
        return 0

    lax.fori_loop(0, tokens // step, project, 0, unroll=2)
    for copy in halos:
        copy.wait()
    edge = dot(halo_ref[...], wi_ref[:, :width]).astype(BF16).astype(F32)
    north, south = row > 0, row < n - 1
    lwest, least = col > 0, col < n - 1

    def seen(slot, ok, first=0, count=tc):
        return jnp.where(ok, edge[slot * tc + first : slot * tc + first + count], 0.0)

    n_all, s_all = seen(0, north), seen(1, south)
    w_all, e_all = seen(2, lwest), seen(3, least)
    nw, ne = seen(4, north & lwest, tc - 8, 8), seen(5, north & least, 0, 8)
    sw, se = seen(6, south & lwest, tc - 8, 8), seen(7, south & least, 0, 8)
    for k in range(groups):
        pad_ref[k, 0, 8 : 8 + tc, :] = n_all[:, cols(k)]
        pad_ref[k, tr + 1, 8 : 8 + tc, :] = s_all[:, cols(k)]
        pad_ref[k, 0, 0:8, :] = nw[:, cols(k)]
        pad_ref[k, 0, 8 + tc : 16 + tc, :] = ne[:, cols(k)]
        pad_ref[k, tr + 1, 0:8, :] = sw[:, cols(k)]
        pad_ref[k, tr + 1, 8 + tc : 16 + tc, :] = se[:, cols(k)]
        for r in range(tr):
            pad_ref[k, 1 + r, 7:8, :] = w_all[r : r + 1, cols(k)]
            pad_ref[k, 1 + r, 8 + tc : 9 + tc, :] = e_all[r : r + 1, cols(k)]
    fetch[3].wait()
    fetch[4].wait()
    bias = cb_ref[...].reshape(1, width)

    def row_tokens(r, to, which, owner):
        return remote(
            act_ref.at[r], line_ref.at[0, tile(which * half + owner)], ts_sem.at[0, r],
            tr_sem.at[0, which * half + owner], row, side * half + to,
        )

    def column_tokens(step, peer, owner):
        return remote(actt_ref.at[peer], line_ref.at[1, tile(owner)], ts_sem.at[1, step], tr_sem.at[1, owner], peer, col)

    def convolve(i, _):
        r = lax.rem(2 * seat + i, n)
        for k in range(groups):
            total = jnp.broadcast_to(bias[:, cols(k)], (tc, LANES))
            for a in range(3):
                for b in range(3):
                    total = total + pad_ref[k, r + a, 7 + b : 7 + b + tc, :] * cw_ref[a, b : b + 1, cols(k)]
            done = silu(total).astype(BF16)
            act_ref[r, :, cols(k)] = done
            actf_ref[k, tile(r), :] = done.astype(F32)

        @pl.when(i < n)
        def _():
            row_tokens(r, r // 2, lax.rem(r, 2), seat).start()

        return 0

    lax.fori_loop(2, n + 2, convolve, 0, unroll=2)

    def flip(j, _):
        for k in range(groups):
            actt_ref[j, :, cols(k)] = actf_ref[k, pl.ds(j, tr, stride=tc), :].astype(BF16)
        return 0

    lax.fori_loop(0, tc, flip, 0, unroll=4)
    others(lambda step, peer: column_tokens(step, peer, row).start())
    for which in range(2):
        line_ref[0, tile(which * half + seat), :] = act_ref[2 * seat + which]
    line_ref[1, tile(row), :] = actt_ref[row]

    def gates(i, _):
        at = pl.ds(pl.multiple_of(i * step, step), step)
        gate = dot(nb_ref[at, :], wi_ref[:, width:]).astype(BF16).astype(F32)
        gate_ref[at, :] = silu(gate)
        return 0

    lax.fori_loop(0, tokens // step, gates, 0, unroll=2)
    for i in range(5, len(fetch)):
        fetch[i].wait()

    def rates(d, _):
        for k in range(groups):
            dec_ref[d, k] = jnp.exp(dl_ref[d, :, cols(k)]) * -LOG2E
        return 0

    lax.fori_loop(0, dl_ref.shape[0], rates, 0)

    span = 16
    blocks = length // span
    held = (ha_ref, hb_ref)
    kk, cc = iota((3 * rank + states, span * states), 0), iota((3 * rank + states, span * states), 1)
    lane = iota((states, LANES), 1)

    def ready(line):
        def prepare(d, _):
            which = line * 2 + d
            repeat = (kk == 3 * rank + lax.rem(cc, states)).astype(BF16)
            slot = iota((length, span * states), 1) // states
            mask = lax.rem(iota((length, span * states), 0), span) == slot + d * (span - 1 - 2 * slot)
            u = line_ref[line]
            to_rank = pw_ref[which, :rank, :]
            p = dot_nt(u, jnp.concatenate([to_rank] * 3 + [pw_ref[which, rank + states :, :]], axis=0))
            high = p.astype(BF16)
            low = p - high.astype(F32)
            stacked = jnp.where(iota(p.shape, 1) < 2 * rank, high.astype(F32), low).astype(BF16)[:, : 3 * rank]
            mc_ref[line, d] = jnp.where(mask, dot(high, repeat), 0.0).astype(BF16)
            weight = sw_ref[which]
            swh = weight.astype(BF16)
            swl = (weight - swh.astype(F32)).astype(BF16)
            weights = jnp.concatenate([swh, swl, swh], axis=0)
            shift = sb_ref[pl.ds(which, 1), :]
            wide = PIECE * LANES
            for g in range(0, groups, PIECE):
                at = slice(g * LANES, g * LANES + wide)
                s = softplus(dot(stacked, weights[:, at]) + shift[:, at])
                du = s * line_ref[line, :, at].astype(F32)
                for k in range(PIECE):
                    s_ref[line, d, g + k] = s[:, cols(k)]
                    du_ref[line, d, g + k] = du[:, cols(k)]
            enter = dot_nt(pw_ref[which, rank : rank + states, :], u)
            ones = jnp.ones((LANES, LANES), BF16)
            for h in range(length // LANES):
                for g in range(0, LANES, span):
                    spread = [jnp.where(lane == g + i, enter[:, cols(h)], 0.0) for i in range(span)]
                    at = (h * LANES + g) * states
                    bb_ref[line, d, at : at + span * states, :] = dot(jnp.concatenate(spread, axis=0).astype(BF16), ones)
            return 0

        lax.fori_loop(0, 2, prepare, 0)
        skip = sk_ref[pl.ds(line * 2, 1), :] + sk_ref[pl.ds(line * 2 + 1, 1), :]

        def begin(i, _):
            at = pl.ds(pl.multiple_of(i * 32, 32), 32)
            v = line_ref[line, at, :].astype(F32) * skip
            for k in range(groups):
                acc_ref[line, k, at, :] = v[:, cols(k)]
            return 0

        lax.fori_loop(0, length // 32, begin, 0, unroll=2)

    def zeros(per):
        return tuple(tuple((jnp.zeros((8, LANES), F32),) * 2 for _ in range(per)) for _ in range(2))

    def run(line, per, g0, streams, blocks, init):
        dec = [
            [[dec_ref[w, g0 + k, 8 * v : 8 * v + 8, :] for v in range(2)] for k in range(per)] for w, _, _, _ in streams
        ]

        def low(i, q):
            _, _, first, back = streams[q]
            return pl.multiple_of(first + (i + back * (blocks - 1 - 2 * i)) * span, span)

        def leave(slot, i, q, spare=None):
            b = low(i, q)
            to = b if spare is None else jnp.where(spare, length, b)
            to = pl.multiple_of(to, span)
            states_now = jnp.concatenate([held[slot][q, k] for k in range(per)], axis=1)
            part = dot(mc_ref[line, streams[q][1], pl.ds(b, span), :], states_now)
            for k in range(per):
                acc_ref[line, g0 + k, pl.ds(to, span), :] += part[:, cols(k)]

        def advance(slot, i, h):
            for j in range(span):
                for q in range(2):
                    _, d, _, back = streams[q]
                    t = low(i, q) + (j + back * (span - 1 - 2 * j))
                    enter = [bb_ref[line, d, pl.ds(pl.multiple_of(t * states + 8 * v, 8), 8), :] for v in range(2)]
                    for k in range(per):
                        s = s_ref[line, d, g0 + k, pl.ds(t, 8, stride=0), :]
                        du = du_ref[line, d, g0 + k, pl.ds(t, 8, stride=0), :]
                        now = [jnp.exp2(s * dec[q][k][v]) * h[q][k][v] + du * enter[v] for v in range(2)]
                        h[q][k] = now
                        held[slot][q, k, j * states : (j + 1) * states, :] = jnp.concatenate(now, axis=0).astype(BF16)
            return h

        def body(i, h):
            h = [[list(v) for v in part] for part in h]
            for q in range(2):
                leave(1, jnp.maximum(2 * i - 1, 0), q, i == 0)
            h = advance(0, 2 * i, h)
            for q in range(2):
                leave(0, 2 * i, q)
            h = advance(1, 2 * i + 1, h)
            return tuple(tuple(tuple(v) for v in part) for part in h)

        h = lax.fori_loop(0, blocks // 2, body, init)
        for q in range(2):
            leave(1, blocks - 1, q)
        return h

    def settle(line, per, g0):
        for k in range(per):
            y_ref[line, g0 + k] = acc_ref[line, g0 + k, :length].astype(BF16)

    def row_result(c, r, to, which, owner):
        at = pl.ds(c * PER[0], PER[0])
        return remote(
            y_ref.at[0, at, tile(which * half + to)], land_ref.at[0, at, 2 * owner + which], ys_sem.at[0, c, r],
            yr_sem.at[0, c, 2 * owner + which], row, side * half + to,
        )

    def column_result(c, step, peer, owner):
        at = pl.ds(c * PER[1], PER[1])
        return remote(
            y_ref.at[1, at, tile(peer)], land_ref.at[1, at, owner], ys_sem.at[1, c, step], yr_sem.at[1, c, owner],
            peer, col,
        )

    def state_copy(c):
        return remote(st_ref.at[c], sl_ref.at[c], ss_sem.at[c], sr_sem.at[c], row, lax.rem(col + half, n))

    def lines(d):
        return [(d, d, which * (length // 2), d) for which in range(2)]

    def outward(c, _):
        per = PER[0]
        h = run(0, per, c * per, lines(side), blocks // 2, zeros(per))
        for q in range(2):
            for k in range(per):
                st_ref[c, q, k] = jnp.concatenate(h[q][k], axis=0).astype(BF16)
        state_copy(c).start()
        return 0

    def inward(c, _):
        per = PER[0]
        state_copy(c).wait_recv()
        came = [[sl_ref[c, q, k].astype(F32) for k in range(per)] for q in range(2)]
        init = tuple(tuple((v[:8], v[8:]) for v in part) for part in came)
        run(0, per, c * per, lines(1 - side), blocks // 2, init)
        settle(0, per, c * per)
        mates(lambda r, to, which: row_result(c, r, to, which, seat).start())
        for k in range(per):
            for which in range(2):
                land_ref[0, c * per + k, 2 * seat + which] = y_ref[0, c * per + k, tile(which * half + seat), :]
        return 0

    def down_and_up(c, _):
        per = PER[1]
        run(1, per, c * per, [(2, 0, 0, 0), (3, 1, 0, 1)], blocks, zeros(per))
        settle(1, per, c * per)
        others(lambda step, peer: column_result(c, step, peer, row).start())
        for k in range(per):
            land_ref[1, c * per + k, row] = y_ref[1, c * per + k, tile(row), :]
        return 0

    mates(lambda r, to, which: row_tokens(r, to, which, to).wait_recv())
    ready(0)
    lax.fori_loop(0, groups // PER[0], outward, 0)
    others(lambda step, peer: column_tokens(step, peer, peer).wait_recv())
    ready(1)
    lax.fori_loop(0, groups // PER[1], down_and_up, 0)
    lax.fori_loop(0, groups // PER[0], inward, 0)
    for c in range(groups // PER[1]):
        others(lambda step, peer: column_result(c, step, peer, peer).wait_recv())

        def widen(j, _):
            for k in range(c * PER[1], (c + 1) * PER[1]):
                cf_ref[k, tile(j), :] = land_ref[1, k, j].astype(F32)
            return 0

        lax.fori_loop(0, tc, widen, 0, unroll=4)

    for c in range(groups // PER[0]):
        mates(lambda r, to, which: row_result(c, r, to, which, to).wait_recv())

    def finish(r, _):
        other = jnp.concatenate([cf_ref[k, pl.ds(r, tc, stride=tr), :] for k in range(groups)], axis=1)
        v = jnp.concatenate([land_ref[0, k, r] for k in range(groups)], axis=1).astype(F32) + other
        v = v - jnp.mean(v, axis=-1, keepdims=True)
        v = v * lax.rsqrt(jnp.mean(v * v, axis=-1, keepdims=True) + 1e-05) * og_ref[...].reshape(1, width)
        go_ref[tile(r), :] = (v * gate_ref[tile(r), :]).astype(BF16)
        return 0

    lax.fori_loop(0, tr, finish, 0, unroll=8)
    out_ref[...] = dot(go_ref[...], wo_ref[...]).astype(BF16).reshape(out_ref.shape)

    mates(lambda r, to, which: row_tokens(r, to, which, seat).wait_send())
    others(lambda step, peer: column_tokens(step, peer, row).wait_send())
    for c in range(groups // PER[0]):
        state_copy(c).wait_send()
        mates(lambda r, to, which: row_result(c, r, to, which, seat).wait_send())
    for c in range(groups // PER[1]):
        others(lambda step, peer: column_result(c, step, peer, row).wait_send())


def local(
    n, features, norm_gain, in_weight, conv_weight, conv_bias, proj_weight, step_weight, step_bias,
    decay_log, skip_gain, out_gain, out_weight,
):
    tr, tc, channels = features.shape
    width = out_weight.shape[0]
    tokens = tr * tc
    groups = width // LANES
    length = tc * n
    dma = pltpu.SemaphoreType.DMA
    pw = jnp.swapaxes(proj_weight, 1, 2)
    dl = jnp.swapaxes(decay_log, 1, 2)
    states = dl.shape[1]
    span, per = 16, max(PER)
    chunks = groups // min(PER)
    hbm = pl.BlockSpec(memory_space=pltpu.HBM)
    operands = (
        features, norm_gain, in_weight, conv_weight, conv_bias, pw, step_weight, step_bias, dl, skip_gain,
        out_gain, out_weight,
    )
    return pl.pallas_call(
        functools.partial(block_kernel, n),
        out_shape=jax.ShapeDtypeStruct(features.shape, BF16),
        in_specs=[hbm] * len(operands),
        out_specs=VMEM,
        scratch_shapes=[pltpu.VMEM(a.shape, a.dtype) for a in operands] + [
            pltpu.VMEM((tokens, channels), BF16),
            pltpu.VMEM((channels // LANES, tokens, LANES), F32),
            pltpu.VMEM((2, tr, channels), BF16),
            pltpu.VMEM((8 * tc, channels), BF16),
            pltpu.VMEM((groups, tr + 2, tc + 16, LANES), F32),
            pltpu.VMEM((tr, tc, width), BF16),
            pltpu.VMEM((tc, tr, width), BF16),
            pltpu.VMEM((groups, tokens, LANES), F32),
            pltpu.VMEM((2, length, width), BF16),
            pltpu.VMEM((tokens, width), F32),
            pltpu.VMEM((2, 2, groups, length, LANES), F32),
            pltpu.VMEM((2, 2, groups, length, LANES), F32),
            pltpu.VMEM((2, 2, length * states, LANES), F32),
            pltpu.VMEM((2, 2, length, span * states), BF16),
            pltpu.VMEM((dl.shape[0], groups, states, LANES), F32),
            pltpu.VMEM((2, per, span * states, LANES), BF16),
            pltpu.VMEM((2, per, span * states, LANES), BF16),
            pltpu.VMEM((2, groups, length + span, LANES), F32),
            pltpu.VMEM((2, groups, length, LANES), BF16),
            pltpu.VMEM((2, groups, n, tc, LANES), BF16),
            pltpu.VMEM((groups, tokens, LANES), F32),
            pltpu.VMEM((tokens, width), BF16),
            pltpu.VMEM((groups // PER[0], 2, PER[0], states, LANES), BF16),
            pltpu.VMEM((groups // PER[0], 2, PER[0], states, LANES), BF16),
            dma((len(operands),)), dma((8,)), dma((8,)), dma((2, n)), dma((2, n)), dma((2, chunks, n)), dma((2, chunks, n)),
            dma((groups // PER[0],)), dma((groups // PER[0],)),
        ],
        compiler_params=pltpu.CompilerParams(collective_id=0, has_side_effects=True, vmem_limit_bytes=60 << 20),
    )(*operands)


def solution(mesh):
    n = mesh.shape["row"]
    assert mesh.shape["col"] == n
    in_specs = (P("row", "col", None), P(), P(), P(), P(), P(), P(), P(), P(), P(), P(), P())
    return jax.shard_map(
        functools.partial(local, n), mesh=mesh, in_specs=in_specs, out_specs=P("row", "col", None), check_vma=False
    )
```

```python
import functools

import jax
import jax.numpy as jnp
from jax import lax
from jax.experimental import pallas as pl
from jax.experimental.pallas import tpu as pltpu
from jax.sharding import PartitionSpec as P

F32 = jnp.float32
BF16 = jnp.bfloat16
MESH = pl.DeviceIdType.MESH
NT = (((1,), (1,)), ((), ()))
LANES = 128
LOG2E = 1.4426950408889634
PIECE = 2
PER = (3, 3)
VMEM = pl.BlockSpec(memory_space=pltpu.VMEM)


def dot(a, b):
    return jnp.dot(a, b, preferred_element_type=F32)


def dot_nt(a, b):
    return lax.dot_general(a, b, NT, preferred_element_type=F32)


def softplus(z):
    w = jnp.exp2(jnp.abs(z) * -LOG2E)
    small = w * (1.0 - w * (0.5 - w * (1.0 / 3.0)))
    return jnp.maximum(z, 0.0) + jnp.where(w < 0.01, small, jnp.log(1.0 + w))


def silu(v):
    return v / (1.0 + jnp.exp(-v))


def iota(shape, dim):
    return lax.broadcasted_iota(jnp.int32, shape, dim)


def cols(k):
    return slice(k * LANES, (k + 1) * LANES)


def place():
    return lax.axis_index("row"), lax.axis_index("col")


def greet(nr, nc):
    row, col = place()
    sem = pltpu.get_barrier_semaphore()

    def signal(r, c):
        pl.semaphore_signal(sem, inc=1, device_id={"row": r, "col": c}, device_id_type=MESH)

    def along_col(k, _):
        signal(row, lax.rem(col + k, nc))
        return 0

    def along_row(k, _):
        signal(lax.rem(row + k, nr), col)
        return 0

    lax.fori_loop(1, nc, along_col, 0)
    lax.fori_loop(1, nr, along_row, 0)
    for dr in (1, nr - 1):
        for dc in (1, nc - 1):
            signal(lax.rem(row + dr, nr), lax.rem(col + dc, nc))
    return lambda: pl.semaphore_wait(sem, nr + nc + 2)


def remote(src, dst, send_sem, recv_sem, r, c):
    return pltpu.make_async_remote_copy(
        src_ref=src, dst_ref=dst, send_sem=send_sem, recv_sem=recv_sem,
        device_id={"row": r, "col": c}, device_id_type=MESH,
    )


def block_kernel(
    n, x_hbm, gain_hbm, wi_hbm, cw_hbm, cb_hbm, pw_hbm, sw_hbm, sb_hbm, dl_hbm, sk_hbm, og_hbm, wo_hbm, out_ref,
    x_ref, gain_ref, wi_ref, cw_ref, cb_ref, pw_ref, sw_ref, sb_ref, dl_ref, sk_ref, og_ref, wo_ref,
    nb_ref, nf_ref, strip_ref, halo_ref, pad_ref, act_ref, actt_ref, actf_ref, line_ref, gate_ref,
    s_ref, du_ref, bb_ref, mc_ref, dec_ref, ha_ref, hb_ref, acc_ref, y_ref, land_ref, cf_ref, go_ref,
    st_ref, sl_ref, own_sem, hs_sem, hr_sem, ts_sem, tr_sem, ys_sem, yr_sem, ss_sem, sr_sem,
):
    tr, tc, channels = x_ref.shape
    width = cb_ref.shape[-1]
    tokens = tr * tc
    groups = width // LANES
    length = line_ref.shape[1]
    rank, states = sw_ref.shape[1], dl_ref.shape[1]
    row, col = place()
    there = (x_hbm, gain_hbm, wi_hbm, cw_hbm, cb_hbm, pw_hbm, sw_hbm, sb_hbm, dl_hbm, sk_hbm, og_hbm, wo_hbm)
    here = (x_ref, gain_ref, wi_ref, cw_ref, cb_ref, pw_ref, sw_ref, sb_ref, dl_ref, sk_ref, og_ref, wo_ref)
    fetch = [pltpu.make_async_copy(src, dst, own_sem.at[i]) for i, (src, dst) in enumerate(zip(there, here))]
    fetch[0].start()
    greeted = greet(n, n)
    for copy in fetch[1:]:
        copy.start()

    half = n // 2
    side, seat = col // half, lax.rem(col, half)

    def others(one):
        def body(step, _):
            one(step, lax.rem(row + step, n))
            return 0

        lax.fori_loop(1, n, body, 0)

    def mates(one):
        def body(step, _):
            r = lax.rem(2 * seat + step, n)
            one(r, r // 2, lax.rem(r, 2))
            return 0

        lax.fori_loop(2, n, body, 0)

    def tile(i):
        return pl.ds(pl.multiple_of(i * tc, tc), tc)

    step = 4 * tc
    fetch[0].wait()
    fetch[1].wait()

    def norm(i, _):
        v = x_ref[pl.ds(i * 4, 4)].reshape(step, channels).astype(F32)
        v = v - jnp.mean(v, axis=-1, keepdims=True)
        v = v * lax.rsqrt(jnp.mean(v * v, axis=-1, keepdims=True) + 1e-05) * gain_ref[...].reshape(1, channels)
        at = pl.ds(pl.multiple_of(i * step, step), step)
        nb_ref[at, :] = v.astype(BF16)
        for k in range(channels // LANES):
            nf_ref[k, at, :] = v[:, cols(k)]
        return 0

    hb_ref[...] = jnp.zeros_like(hb_ref)
    lax.fori_loop(0, tokens // step, norm, 0, unroll=4)
    for k in range(channels // LANES):
        strip_ref[0, :, cols(k)] = nf_ref[k, pl.ds(0, tr, stride=tc), :].astype(BF16)
        strip_ref[1, :, cols(k)] = nf_ref[k, pl.ds(tc - 1, tr, stride=tc), :].astype(BF16)
    top, bottom = nb_ref.at[pl.ds(0, tc)], nb_ref.at[pl.ds(tokens - tc, tc)]
    left, right = strip_ref.at[0], strip_ref.at[1]
    up, down = lax.rem(row + n - 1, n), lax.rem(row + 1, n)
    west, east = lax.rem(col + n - 1, n), lax.rem(col + 1, n)
    greeted()
    plan = (
        (bottom, down, col), (top, up, col), (right, row, east), (left, row, west),
        (bottom, down, east), (bottom, down, west), (top, up, east), (top, up, west),
    )
    halos = [
        remote(src, halo_ref.at[pl.ds(slot * tc, tc)], hs_sem.at[slot], hr_sem.at[slot], r, c)
        for slot, (src, r, c) in enumerate(plan)
    ]
    for copy in halos:
        copy.start()
    fetch[2].wait()

    def project(i, _):
        at = pl.ds(pl.multiple_of(i * step, step), step)
        inner = dot(nb_ref[at, :], wi_ref[:, :width]).astype(BF16).astype(F32)
        for k in range(groups):
            pad_ref[k, pl.ds(1 + i * 4, 4), 8 : 8 + tc, :] = inner[:, cols(k)].reshape(4, tc, LANES)
        return 0

    lax.fori_loop(0, tokens // step, project, 0, unroll=2)
    for copy in halos:
        copy.wait()
    edge = dot(halo_ref[...], wi_ref[:, :width]).astype(BF16).astype(F32)
    north, south = row > 0, row < n - 1
    lwest, least = col > 0, col < n - 1

    def seen(slot, ok, first=0, count=tc):
        return jnp.where(ok, edge[slot * tc + first : slot * tc + first + count], 0.0)

    n_all, s_all = seen(0, north), seen(1, south)
    w_all, e_all = seen(2, lwest), seen(3, least)
    nw, ne = seen(4, north & lwest, tc - 8, 8), seen(5, north & least, 0, 8)
    sw, se = seen(6, south & lwest, tc - 8, 8), seen(7, south & least, 0, 8)
    for k in range(groups):
        pad_ref[k, 0, 8 : 8 + tc, :] = n_all[:, cols(k)]
        pad_ref[k, tr + 1, 8 : 8 + tc, :] = s_all[:, cols(k)]
        pad_ref[k, 0, 0:8, :] = nw[:, cols(k)]
        pad_ref[k, 0, 8 + tc : 16 + tc, :] = ne[:, cols(k)]
        pad_ref[k, tr + 1, 0:8, :] = sw[:, cols(k)]
        pad_ref[k, tr + 1, 8 + tc : 16 + tc, :] = se[:, cols(k)]
        for r in range(tr):
            pad_ref[k, 1 + r, 7:8, :] = w_all[r : r + 1, cols(k)]
            pad_ref[k, 1 + r, 8 + tc : 9 + tc, :] = e_all[r : r + 1, cols(k)]
    fetch[3].wait()
    fetch[4].wait()
    bias = cb_ref[...].reshape(1, width)

    def row_tokens(r, to, which, owner):
        return remote(
            act_ref.at[r], line_ref.at[0, tile(which * half + owner)], ts_sem.at[0, r],
            tr_sem.at[0, which * half + owner], row, side * half + to,
        )

    def column_tokens(step, peer, owner):
        return remote(actt_ref.at[peer], line_ref.at[1, tile(owner)], ts_sem.at[1, step], tr_sem.at[1, owner], peer, col)

    def convolve(i, _):
        r = lax.rem(2 * seat + i, n)
        for k in range(groups):
            total = jnp.broadcast_to(bias[:, cols(k)], (tc, LANES))
            for a in range(3):
                for b in range(3):
                    total = total + pad_ref[k, r + a, 7 + b : 7 + b + tc, :] * cw_ref[a, b : b + 1, cols(k)]
            done = silu(total).astype(BF16)
            act_ref[r, :, cols(k)] = done
            actf_ref[k, tile(r), :] = done.astype(F32)

        @pl.when(i < n)
        def _():
            row_tokens(r, r // 2, lax.rem(r, 2), seat).start()

        return 0

    lax.fori_loop(2, n + 2, convolve, 0, unroll=4)

    def flip(j, _):
        for k in range(groups):
            actt_ref[j, :, cols(k)] = actf_ref[k, pl.ds(j, tr, stride=tc), :].astype(BF16)
        return 0

    lax.fori_loop(0, tc, flip, 0, unroll=4)
    others(lambda step, peer: column_tokens(step, peer, row).start())
    for which in range(2):
        line_ref[0, tile(which * half + seat), :] = act_ref[2 * seat + which]
    line_ref[1, tile(row), :] = actt_ref[row]

    def gates(i, _):
        at = pl.ds(pl.multiple_of(i * step, step), step)
        gate = dot(nb_ref[at, :], wi_ref[:, width:]).astype(BF16).astype(F32)
        gate_ref[at, :] = silu(gate)
        return 0

    lax.fori_loop(0, tokens // step, gates, 0, unroll=2)
    for i in range(5, len(fetch)):
        fetch[i].wait()

    def rates(d, _):
        for k in range(groups):
            dec_ref[d, k] = jnp.exp(dl_ref[d, :, cols(k)]) * -LOG2E
        return 0

    lax.fori_loop(0, dl_ref.shape[0], rates, 0, unroll=2)

    span = 16
    blocks = length // span
    held = (ha_ref, hb_ref)
    kk, cc = iota((3 * rank + states, span * states), 0), iota((3 * rank + states, span * states), 1)
    lane = iota((states, LANES), 1)

    def ready(line):
        def prepare(d, _):
            which = line * 2 + d
            repeat = (kk == 3 * rank + lax.rem(cc, states)).astype(BF16)
            slot = iota((length, span * states), 1) // states
            mask = lax.rem(iota((length, span * states), 0), span) == slot + d * (span - 1 - 2 * slot)
            u = line_ref[line]
            to_rank = pw_ref[which, :rank, :]
            p = dot_nt(u, jnp.concatenate([to_rank] * 3 + [pw_ref[which, rank + states :, :]], axis=0))
            high = p.astype(BF16)
            low = p - high.astype(F32)
            stacked = jnp.where(iota(p.shape, 1) < 2 * rank, high.astype(F32), low).astype(BF16)[:, : 3 * rank]
            mc_ref[line, d] = jnp.where(mask, dot(high, repeat), 0.0).astype(BF16)
            weight = sw_ref[which]
            swh = weight.astype(BF16)
            swl = (weight - swh.astype(F32)).astype(BF16)
            weights = jnp.concatenate([swh, swl, swh], axis=0)
            shift = sb_ref[pl.ds(which, 1), :]
            wide = PIECE * LANES
            for g in range(0, groups, PIECE):
                at = slice(g * LANES, g * LANES + wide)
                s = softplus(dot(stacked, weights[:, at]) + shift[:, at])
                du = s * line_ref[line, :, at].astype(F32)
                for k in range(PIECE):
                    s_ref[line, d, g + k] = s[:, cols(k)]
                    du_ref[line, d, g + k] = du[:, cols(k)]
            enter = dot_nt(pw_ref[which, rank : rank + states, :], u)
            ones = jnp.ones((LANES, LANES), BF16)
            for h in range(length // LANES):
                for g in range(0, LANES, span):
                    spread = [jnp.where(lane == g + i, enter[:, cols(h)], 0.0) for i in range(span)]
                    at = (h * LANES + g) * states
                    bb_ref[line, d, at : at + span * states, :] = dot(jnp.concatenate(spread, axis=0).astype(BF16), ones)
            return 0

        lax.fori_loop(0, 2, prepare, 0, unroll=2)
        skip = sk_ref[pl.ds(line * 2, 1), :] + sk_ref[pl.ds(line * 2 + 1, 1), :]

        def begin(i, _):
            at = pl.ds(pl.multiple_of(i * 32, 32), 32)
            v = line_ref[line, at, :].astype(F32) * skip
            for k in range(groups):
                acc_ref[line, k, at, :] = v[:, cols(k)]
            return 0

        lax.fori_loop(0, length // 32, begin, 0, unroll=2)

    def zeros(per):
        return tuple(tuple((jnp.zeros((8, LANES), F32),) * 2 for _ in range(per)) for _ in range(2))

    def run(line, per, g0, streams, blocks, init):
        dec = [
            [[dec_ref[w, g0 + k, 8 * v : 8 * v + 8, :] for v in range(2)] for k in range(per)] for w, _, _, _ in streams
        ]

        def low(i, q):
            _, _, first, back = streams[q]
            return pl.multiple_of(first + (i + back * (blocks - 1 - 2 * i)) * span, span)

        def leave(slot, i, q, spare=None):
            b = low(i, q)
            to = b if spare is None else jnp.where(spare, length, b)
            to = pl.multiple_of(to, span)
            states_now = jnp.concatenate([held[slot][q, k] for k in range(per)], axis=1)
            part = dot(mc_ref[line, streams[q][1], pl.ds(b, span), :], states_now)
            for k in range(per):
                acc_ref[line, g0 + k, pl.ds(to, span), :] += part[:, cols(k)]

        def advance(slot, i, h):
            for j in range(span):
                for q in range(2):
                    _, d, _, back = streams[q]
                    t = low(i, q) + (j + back * (span - 1 - 2 * j))
                    enter = [bb_ref[line, d, pl.ds(pl.multiple_of(t * states + 8 * v, 8), 8), :] for v in range(2)]
                    for k in range(per):
                        s = s_ref[line, d, g0 + k, pl.ds(t, 8, stride=0), :]
                        du = du_ref[line, d, g0 + k, pl.ds(t, 8, stride=0), :]
                        now = [jnp.exp2(s * dec[q][k][v]) * h[q][k][v] + du * enter[v] for v in range(2)]
                        h[q][k] = now
                        held[slot][q, k, j * states : (j + 1) * states, :] = jnp.concatenate(now, axis=0).astype(BF16)
            return h

        def body(i, h):
            h = [[list(v) for v in part] for part in h]
            for q in range(2):
                leave(1, jnp.maximum(2 * i - 1, 0), q, i == 0)
            h = advance(0, 2 * i, h)
            for q in range(2):
                leave(0, 2 * i, q)
            h = advance(1, 2 * i + 1, h)
            return tuple(tuple(tuple(v) for v in part) for part in h)

        h = lax.fori_loop(0, blocks // 2, body, init)
        for q in range(2):
            leave(1, blocks - 1, q)
        return h

    def settle(line, per, g0):
        for k in range(per):
            y_ref[line, g0 + k] = acc_ref[line, g0 + k, :length].astype(BF16)

    def row_result(c, r, to, which, owner):
        at = pl.ds(c * PER[0], PER[0])
        return remote(
            y_ref.at[0, at, tile(which * half + to)], land_ref.at[0, at, 2 * owner + which], ys_sem.at[0, c, r],
            yr_sem.at[0, c, 2 * owner + which], row, side * half + to,
        )

    def column_result(c, step, peer, owner):
        at = pl.ds(c * PER[1], PER[1])
        return remote(
            y_ref.at[1, at, tile(peer)], land_ref.at[1, at, owner], ys_sem.at[1, c, step], yr_sem.at[1, c, owner],
            peer, col,
        )

    def state_copy(c):
        return remote(st_ref.at[c], sl_ref.at[c], ss_sem.at[c], sr_sem.at[c], row, lax.rem(col + half, n))

    def lines(d):
        return [(d, d, which * (length // 2), d) for which in range(2)]

    def outward(c, _):
        per = PER[0]
        h = run(0, per, c * per, lines(side), blocks // 2, zeros(per))
        for q in range(2):
            for k in range(per):
                st_ref[c, q, k] = jnp.concatenate(h[q][k], axis=0).astype(BF16)
        state_copy(c).start()
        return 0

    def inward(c, _):
        per = PER[0]
        state_copy(c).wait_recv()
        came = [[sl_ref[c, q, k].astype(F32) for k in range(per)] for q in range(2)]
        init = tuple(tuple((v[:8], v[8:]) for v in part) for part in came)
        run(0, per, c * per, lines(1 - side), blocks // 2, init)
        settle(0, per, c * per)
        mates(lambda r, to, which: row_result(c, r, to, which, seat).start())
        for k in range(per):
            for which in range(2):
                land_ref[0, c * per + k, 2 * seat + which] = y_ref[0, c * per + k, tile(which * half + seat), :]
        return 0

    def down_and_up(c, _):
        per = PER[1]
        run(1, per, c * per, [(2, 0, 0, 0), (3, 1, 0, 1)], blocks, zeros(per))
        settle(1, per, c * per)
        others(lambda step, peer: column_result(c, step, peer, row).start())
        for k in range(per):
            land_ref[1, c * per + k, row] = y_ref[1, c * per + k, tile(row), :]
        return 0

    mates(lambda r, to, which: row_tokens(r, to, which, to).wait_recv())
    ready(0)
    lax.fori_loop(0, groups // PER[0], outward, 0)
    others(lambda step, peer: column_tokens(step, peer, peer).wait_recv())
    ready(1)
    lax.fori_loop(0, groups // PER[1], down_and_up, 0)
    lax.fori_loop(0, groups // PER[0], inward, 0)
    for c in range(groups // PER[1]):
        others(lambda step, peer: column_result(c, step, peer, peer).wait_recv())

        def widen(j, _):
            for k in range(c * PER[1], (c + 1) * PER[1]):
                cf_ref[k, tile(j), :] = land_ref[1, k, j].astype(F32)
            return 0

        lax.fori_loop(0, tc, widen, 0, unroll=4)

    for c in range(groups // PER[0]):
        mates(lambda r, to, which: row_result(c, r, to, which, to).wait_recv())

    def finish(r, _):
        other = jnp.concatenate([cf_ref[k, pl.ds(r, tc, stride=tr), :] for k in range(groups)], axis=1)
        v = jnp.concatenate([land_ref[0, k, r] for k in range(groups)], axis=1).astype(F32) + other
        v = v - jnp.mean(v, axis=-1, keepdims=True)
        v = v * lax.rsqrt(jnp.mean(v * v, axis=-1, keepdims=True) + 1e-05) * og_ref[...].reshape(1, width)
        go_ref[tile(r), :] = (v * gate_ref[tile(r), :]).astype(BF16)
        return 0

    lax.fori_loop(0, tr, finish, 0, unroll=16)
    out_ref[...] = dot(go_ref[...], wo_ref[...]).astype(BF16).reshape(out_ref.shape)

    mates(lambda r, to, which: row_tokens(r, to, which, seat).wait_send())
    others(lambda step, peer: column_tokens(step, peer, row).wait_send())
    for c in range(groups // PER[0]):
        state_copy(c).wait_send()
        mates(lambda r, to, which: row_result(c, r, to, which, seat).wait_send())
    for c in range(groups // PER[1]):
        others(lambda step, peer: column_result(c, step, peer, row).wait_send())


def local(
    n, features, norm_gain, in_weight, conv_weight, conv_bias, proj_weight, step_weight, step_bias,
    decay_log, skip_gain, out_gain, out_weight,
):
    tr, tc, channels = features.shape
    width = out_weight.shape[0]
    tokens = tr * tc
    groups = width // LANES
    length = tc * n
    dma = pltpu.SemaphoreType.DMA
    pw = jnp.swapaxes(proj_weight, 1, 2)
    dl = jnp.swapaxes(decay_log, 1, 2)
    states = dl.shape[1]
    span, per = 16, max(PER)
    chunks = groups // min(PER)
    hbm = pl.BlockSpec(memory_space=pltpu.HBM)
    operands = (
        features, norm_gain, in_weight, conv_weight, conv_bias, pw, step_weight, step_bias, dl, skip_gain,
        out_gain, out_weight,
    )
    return pl.pallas_call(
        functools.partial(block_kernel, n),
        out_shape=jax.ShapeDtypeStruct(features.shape, BF16),
        in_specs=[hbm] * len(operands),
        out_specs=VMEM,
        scratch_shapes=[pltpu.VMEM(a.shape, a.dtype) for a in operands] + [
            pltpu.VMEM((tokens, channels), BF16),
            pltpu.VMEM((channels // LANES, tokens, LANES), F32),
            pltpu.VMEM((2, tr, channels), BF16),
            pltpu.VMEM((8 * tc, channels), BF16),
            pltpu.VMEM((groups, tr + 2, tc + 16, LANES), F32),
            pltpu.VMEM((tr, tc, width), BF16),
            pltpu.VMEM((tc, tr, width), BF16),
            pltpu.VMEM((groups, tokens, LANES), F32),
            pltpu.VMEM((2, length, width), BF16),
            pltpu.VMEM((tokens, width), F32),
            pltpu.VMEM((2, 2, groups, length, LANES), F32),
            pltpu.VMEM((2, 2, groups, length, LANES), F32),
            pltpu.VMEM((2, 2, length * states, LANES), F32),
            pltpu.VMEM((2, 2, length, span * states), BF16),
            pltpu.VMEM((dl.shape[0], groups, states, LANES), F32),
            pltpu.VMEM((2, per, span * states, LANES), BF16),
            pltpu.VMEM((2, per, span * states, LANES), BF16),
            pltpu.VMEM((2, groups, length + span, LANES), F32),
            pltpu.VMEM((2, groups, length, LANES), BF16),
            pltpu.VMEM((2, groups, n, tc, LANES), BF16),
            pltpu.VMEM((groups, tokens, LANES), F32),
            pltpu.VMEM((tokens, width), BF16),
            pltpu.VMEM((groups // PER[0], 2, PER[0], states, LANES), BF16),
            pltpu.VMEM((groups // PER[0], 2, PER[0], states, LANES), BF16),
            dma((len(operands),)), dma((8,)), dma((8,)), dma((2, n)), dma((2, n)), dma((2, chunks, n)), dma((2, chunks, n)),
            dma((groups // PER[0],)), dma((groups // PER[0],)),
        ],
        compiler_params=pltpu.CompilerParams(collective_id=0, has_side_effects=True, vmem_limit_bytes=60 << 20),
    )(*operands)


def solution(mesh):
    n = mesh.shape["row"]
    assert mesh.shape["col"] == n
    in_specs = (P("row", "col", None), P(), P(), P(), P(), P(), P(), P(), P(), P(), P(), P())
    return jax.shard_map(
        functools.partial(local, n), mesh=mesh, in_specs=in_specs, out_specs=P("row", "col", None), check_vma=False
    )
```
